512 devices in a mesh: seq: 64 (over y, x, core), ch: 8 (over z).
Axes of the slice: x: 4, y: 8, z: 8, core: 2. Of those that a mesh axis runs over, the one named last changes fastest.
Arguments:
- qkv: bfloat16 [16384, 3, 4096], P('seq', None, 'ch'), may hold values from -6 to 6
- short_w: float32 [3, 3, 4096], P(None, None, 'ch'), may hold values from -3 to 3
- skip: float32 [4096], P('ch'), may hold values from -4 to 4
- filt: float32 [16384, 4096], P('seq', 'ch'), may hold values from -4 to 4
Outputs:
- mixed: bfloat16 [16384, 4096], P('seq', 'ch')
The draws below stay inside these ranges and needn't reach their ends.
All inputs are finite; a program needn't handle non-finite values.
Results may differ from the reference program's by a relative error of at most 0.001.
Values may be sent and summed in bfloat16 or wider, within the bound.
A program may use at most 64 MiB of HBM per device.

```python
import math
import jax
import jax.numpy as jnp
from jax import lax

CH = 4096
SHORT = 3
SEQ = 16384
N_CH = 8


def decay_scale(rate):
    return jnp.sqrt(jnp.expm1(-2.0 * rate) / jnp.expm1(-2.0 * rate * SEQ))


def draw_filt(key, part):
    keys = jax.random.split(jax.random.fold_in(key, 7), 7)
    slow_share = 0.5
    slow = jax.random.uniform(keys[0], (CH,)) < slow_share
    slow_rate = jax.random.uniform(keys[1], (CH,), minval=0.1, maxval=2.0) / SEQ
    fast_rate = jnp.exp(jax.random.uniform(keys[2], (CH,), minval=math.log(1.0 / 60.0), maxval=math.log(1.0 / 25.0)))
    rate = jnp.where(slow, slow_rate, fast_rate)
    tail_rate = jax.random.uniform(keys[4], (CH,), minval=0.1, maxval=2.0) / SEQ
    tail_amp = jax.random.uniform(keys[5], (CH,), minval=0.2, maxval=0.4)
    lags = jnp.arange(SEQ, dtype=jnp.float32)[:, None]
    base = jnp.clip(jax.random.normal(keys[3], (SEQ, CH)), -4.0, 4.0)
    tail_base = jnp.clip(jax.random.normal(keys[6], (SEQ, CH)), -4.0, 4.0)
    head = base * jnp.exp(-rate * lags) * decay_scale(rate)
    tail = tail_base * jnp.exp(-tail_rate * lags) * (tail_amp * decay_scale(tail_rate))
    return (head + tail).astype(jnp.float32)


def block_levels(rng, extent, pieces, smallest, top_value):
    level = 1.0
    for axis_at, shards_of in pieces:
        steps = jax.random.uniform(jax.random.fold_in(jax.random.fold_in(rng, 6), axis_at), (shards_of,), jnp.float32, smallest / len(pieces), top_value / len(pieces))
        level = level * jnp.repeat(jnp.exp(steps), extent[axis_at] // shards_of).reshape((-1,) + (1,) * (len(extent) - 1 - axis_at))
    return level


def centred(rng, shape, spread, bound, pieces=(), held_as=jnp.bfloat16):
    array = spread * jax.random.normal(rng, shape, jnp.float32)
    if pieces:
        array = array * block_levels(rng, shape, pieces, -0.22, 0.18)
    return jnp.clip(array, -bound, bound).astype(held_as)


def setup_inputs(seed: int = 0) -> dict:
    arg_keys = jax.random.split(jax.random.key(seed), 5)
    qkv = centred(arg_keys[0], (SEQ, 3, CH), 1.0, 6.0, ((0, 64), (2, 8)))
    short_w = centred(arg_keys[1], (SHORT, 3, CH), 0.5, 3.0, ((2, 8),), jnp.float32)
    skip = centred(arg_keys[2], (CH,), 1.0, 4.0, ((0, 8),), jnp.float32)
    filt = draw_filt(jax.random.fold_in(arg_keys[4], 71), 0)
    return dict(qkv=qkv, short_w=short_w, skip=skip, filt=filt)


def long_conv(pair):
    sig, fil = pair
    length = 2 * SEQ
    sig_spec = jnp.fft.rfft(sig, n=length, axis=0)
    fil_spec = jnp.fft.rfft(fil, n=length, axis=0)
    return jnp.fft.irfft(sig_spec * fil_spec, n=length, axis=0)[:SEQ]


def reference(qkv, short_w, skip, filt):
    wide = qkv.astype(jnp.float32)
    extended = jnp.concatenate([jnp.zeros((SHORT - 1, 3, CH), jnp.float32), wide], axis=0)
    feat = short_w[0] * extended[SHORT - 1:SHORT - 1 + SEQ]
    for tap in range(1, SHORT):
        feat = feat + short_w[tap] * extended[SHORT - 1 - tap:SHORT - 1 - tap + SEQ]
    query = feat[:, 0, :]
    signal = feat[:, 1, :] * feat[:, 2, :]
    block = CH // N_CH

    def grouped(values):
        return values.reshape(SEQ, N_CH, block).transpose(1, 0, 2)

    conv = lax.map(long_conv, (grouped(signal), grouped(filt)))
    conv = conv.transpose(1, 0, 2).reshape(SEQ, CH)
    return (query * (conv + skip * signal)).astype(jnp.bfloat16)
```

```python
import math

import jax
import jax.numpy as jnp
from jax import lax
from jax.sharding import PartitionSpec as P

HIGHEST = lax.Precision.HIGHEST


def shifted(block, axis, distance):
    devices = range(lax.axis_size(axis))
    route = [(i - distance, i) for i in devices if i - distance in devices]
    return lax.ppermute(block, axis, route)


def phase_table(count_out, count_in, modulus, sign):
    out_idx = jnp.arange(count_out, dtype=jnp.int32)[:, None]
    in_idx = jnp.arange(count_in, dtype=jnp.int32)[None, :]
    phase = out_idx * in_idx % modulus
    angles = sign * 2.0 * math.pi / modulus * phase.astype(jnp.float32)
    return jnp.cos(angles), jnp.sin(angles)


def long_conv(pieces):
    blocks, _, group, rows = pieces.shape
    coarse = 2 * blocks
    total = coarse * rows
    half = blocks + 1
    cos1, sin1 = phase_table(half, blocks, coarse, -1.0)
    y_re = jnp.einsum("kd,dsgr->skgr", cos1, pieces, precision=HIGHEST)
    y_im = jnp.einsum("kd,dsgr->skgr", sin1, pieces, precision=HIGHEST)
    tw_cos, tw_sin = phase_table(half, rows, total, -1.0)
    tw_cos = tw_cos[None, :, None, :]
    tw_sin = tw_sin[None, :, None, :]
    y_re, y_im = y_re * tw_cos - y_im * tw_sin, y_re * tw_sin + y_im * tw_cos
    cos2, sin2 = phase_table(rows, rows, rows, -1.0)
    z_re = jnp.einsum("skgr,rm->skgm", y_re, cos2, precision=HIGHEST) - jnp.einsum(
        "skgr,rm->skgm", y_im, sin2, precision=HIGHEST
    )
    z_im = jnp.einsum("skgr,rm->skgm", y_im, cos2, precision=HIGHEST) + jnp.einsum(
        "skgr,rm->skgm", y_re, sin2, precision=HIGHEST
    )
    p_re = z_re[0] * z_re[1] - z_im[0] * z_im[1]
    p_im = z_re[0] * z_im[1] + z_im[0] * z_re[1]
    q_re = jnp.einsum("kgm,mr->kgr", p_re, cos2, precision=HIGHEST) + jnp.einsum(
        "kgm,mr->kgr", p_im, sin2, precision=HIGHEST
    )
    q_im = jnp.einsum("kgm,mr->kgr", p_im, cos2, precision=HIGHEST) - jnp.einsum(
        "kgm,mr->kgr", p_re, sin2, precision=HIGHEST
    )
    tw_cos = tw_cos[0]
    tw_sin = tw_sin[0]
    q_re, q_im = q_re * tw_cos + q_im * tw_sin, q_im * tw_cos - q_re * tw_sin
    weight = jnp.where(
        (jnp.arange(half) == 0) | (jnp.arange(half) == blocks), 1.0, 2.0
    ).astype(jnp.float32) / total
    cos3, sin3 = phase_table(blocks, half, coarse, 1.0)
    cos3 = cos3 * weight[None, :]
    sin3 = sin3 * weight[None, :]
    return jnp.einsum("dk,kgr->dgr", cos3, q_re, precision=HIGHEST) - jnp.einsum(
        "dk,kgr->dgr", sin3, q_im, precision=HIGHEST
    )


def on_device(qkv, short_w, skip, filt):
    rows, _, width = qkv.shape
    taps = short_w.shape[0]
    shards = lax.axis_size("seq")
    group = width // shards
    rim = shifted(qkv[rows - (taps - 1) :], "seq", 1)
    extended = jnp.concatenate([rim, qkv], axis=0).astype(jnp.float32)
    feat = short_w[0] * extended[taps - 1 : taps - 1 + rows]
    for tap in range(1, taps):
        feat = feat + short_w[tap] * extended[taps - 1 - tap : taps - 1 - tap + rows]
    query = feat[:, 0, :]
    signal = feat[:, 1, :] * feat[:, 2, :]
    source = jnp.stack([signal, filt]).reshape(2, rows, shards, group).transpose(2, 0, 3, 1)
    pieces = lax.all_to_all(source, "seq", split_axis=0, concat_axis=0, tiled=True)
    values = long_conv(pieces)
    back = lax.all_to_all(values, "seq", split_axis=0, concat_axis=0, tiled=True)
    conv = back.reshape(width, rows).T
    return (query * (conv + skip * signal)).astype(jnp.bfloat16)


def solution(mesh):
    return jax.shard_map(
        on_device,
        mesh=mesh,
        in_specs=(P("seq", None, "ch"), P(None, None, "ch"), P("ch"), P("seq", "ch")),
        out_specs=P("seq", "ch"),
        check_vma=False,
    )
```

```python
import math

import jax
import jax.numpy as jnp
from jax import lax
from jax.sharding import PartitionSpec as P

PRECISION = lax.Precision.HIGH


def shifted(block, axis, distance):
    devices = range(lax.axis_size(axis))
    route = [(i - distance, i) for i in devices if i - distance in devices]
    return lax.ppermute(block, axis, route)


def phase_table(count_out, count_in, modulus, sign):
    out_idx = jnp.arange(count_out, dtype=jnp.int32)[:, None]
    in_idx = jnp.arange(count_in, dtype=jnp.int32)[None, :]
    phase = out_idx * in_idx % modulus
    angles = sign * 2.0 * math.pi / modulus * phase.astype(jnp.float32)
    return jnp.cos(angles), jnp.sin(angles)


def long_conv(pieces):
    blocks, _, group, rows = pieces.shape
    coarse = 2 * blocks
    total = coarse * rows
    half = blocks + 1
    cos1, sin1 = phase_table(half, blocks, coarse, -1.0)
    y_re = jnp.einsum("kd,dsgr->skgr", cos1, pieces, precision=PRECISION)
    y_im = jnp.einsum("kd,dsgr->skgr", sin1, pieces, precision=PRECISION)
    tw_cos, tw_sin = phase_table(half, rows, total, -1.0)
    tw_cos = tw_cos[None, :, None, :]
    tw_sin = tw_sin[None, :, None, :]
    y_re, y_im = y_re * tw_cos - y_im * tw_sin, y_re * tw_sin + y_im * tw_cos
    cos2, sin2 = phase_table(rows, rows, rows, -1.0)
    z_re = jnp.einsum("skgr,rm->skgm", y_re, cos2, precision=PRECISION) - jnp.einsum(
        "skgr,rm->skgm", y_im, sin2, precision=PRECISION
    )
    z_im = jnp.einsum("skgr,rm->skgm", y_im, cos2, precision=PRECISION) + jnp.einsum(
        "skgr,rm->skgm", y_re, sin2, precision=PRECISION
    )
    p_re = z_re[0] * z_re[1] - z_im[0] * z_im[1]
    p_im = z_re[0] * z_im[1] + z_im[0] * z_re[1]
    q_re = jnp.einsum("kgm,mr->kgr", p_re, cos2, precision=PRECISION) + jnp.einsum(
        "kgm,mr->kgr", p_im, sin2, precision=PRECISION
    )
    q_im = jnp.einsum("kgm,mr->kgr", p_im, cos2, precision=PRECISION) - jnp.einsum(
        "kgm,mr->kgr", p_re, sin2, precision=PRECISION
    )
    tw_cos = tw_cos[0]
    tw_sin = tw_sin[0]
    q_re, q_im = q_re * tw_cos + q_im * tw_sin, q_im * tw_cos - q_re * tw_sin
    weight = jnp.where(
        (jnp.arange(half) == 0) | (jnp.arange(half) == blocks), 1.0, 2.0
    ).astype(jnp.float32) / total
    cos3, sin3 = phase_table(blocks, half, coarse, 1.0)
    cos3 = cos3 * weight[None, :]
    sin3 = sin3 * weight[None, :]
    return jnp.einsum("dk,kgr->dgr", cos3, q_re, precision=PRECISION) - jnp.einsum(
        "dk,kgr->dgr", sin3, q_im, precision=PRECISION
    )


def on_device(qkv, short_w, skip, filt):
    rows, _, width = qkv.shape
    taps = short_w.shape[0]
    shards = lax.axis_size("seq")
    group = width // shards
    rim = shifted(qkv[rows - (taps - 1) :], "seq", 1)
    extended = jnp.concatenate([rim, qkv], axis=0).astype(jnp.float32)
    feat = short_w[0] * extended[taps - 1 : taps - 1 + rows]
    for tap in range(1, taps):
        feat = feat + short_w[tap] * extended[taps - 1 - tap : taps - 1 - tap + rows]
    query = feat[:, 0, :]
    signal = feat[:, 1, :] * feat[:, 2, :]
    source = jnp.stack([signal, filt]).reshape(2, rows, shards, group).transpose(2, 0, 3, 1)
    pieces = lax.all_to_all(source, "seq", split_axis=0, concat_axis=0, tiled=True)
    values = long_conv(pieces)
    back = lax.all_to_all(values, "seq", split_axis=0, concat_axis=0, tiled=True)
    conv = back.reshape(width, rows).T
    return (query * (conv + skip * signal)).astype(jnp.bfloat16)


def solution(mesh):
    return jax.shard_map(
        on_device,
        mesh=mesh,
        in_specs=(P("seq", None, "ch"), P(None, None, "ch"), P("ch"), P("seq", "ch")),
        out_specs=P("seq", "ch"),
        check_vma=False,
    )
```

```python
import functools
import math

import jax
import jax.numpy as jnp
from jax import lax
from jax.experimental import pallas as pl
from jax.experimental.pallas import tpu as pltpu
from jax.sharding import PartitionSpec as P

PRECISION = lax.Precision.HIGHEST


def shifted(block, axis, distance):
    devices = range(lax.axis_size(axis))
    route = [(i - distance, i) for i in devices if i - distance in devices]
    return lax.ppermute(block, axis, route)


def phase_table(count_out, count_in, modulus, sign):
    out_idx = jnp.arange(count_out, dtype=jnp.int32)[:, None]
    in_idx = jnp.arange(count_in, dtype=jnp.int32)[None, :]
    phase = out_idx * in_idx % modulus
    angles = sign * 2.0 * math.pi / modulus * phase.astype(jnp.float32)
    return jnp.cos(angles), jnp.sin(angles)


def exchange_kernel(shards, x_ref, o_ref, send_sem, recv_sem, own_sem):
    me = lax.axis_index("seq")
    row = lax.axis_index("ch")
    mesh_id = pl.DeviceIdType.MESH
    barrier = pltpu.get_barrier_semaphore()

    def peer_of(step):
        return lax.rem(me + 1 + step, shards)

    def greet(step, carry):
        pl.semaphore_signal(barrier, inc=1, device_id=(peer_of(step), row), device_id_type=mesh_id)
        return carry

    lax.fori_loop(0, shards - 1, greet, 0)
    pl.semaphore_wait(barrier, shards - 1)
    own = pltpu.make_async_copy(x_ref.at[me], o_ref.at[me], own_sem)
    own.start()

    def copy_to(peer):
        return pltpu.make_async_remote_copy(
            src_ref=x_ref.at[peer],
            dst_ref=o_ref.at[me],
            send_sem=send_sem.at[peer],
            recv_sem=recv_sem.at[me],
            device_id=(peer, row),
            device_id_type=mesh_id,
        )

    def send(step, carry):
        copy_to(peer_of(step)).start()
        return carry

    lax.fori_loop(0, shards - 1, send, 0)

    def finish(step, carry):
        peer = peer_of(step)
        copy_to(peer).wait_send()
        pltpu.make_async_remote_copy(
            src_ref=x_ref.at[peer],
            dst_ref=o_ref.at[peer],
            send_sem=send_sem.at[peer],
            recv_sem=recv_sem.at[peer],
            device_id=(peer, row),
            device_id_type=mesh_id,
        ).wait_recv()
        return carry

    lax.fori_loop(0, shards - 1, finish, 0)
    own.wait()


def exchange(x, collective_id):
    shards = x.shape[0]
    return pl.pallas_call(
        functools.partial(exchange_kernel, shards),
        out_shape=jax.ShapeDtypeStruct(x.shape, x.dtype),
        in_specs=[pl.BlockSpec(memory_space=pl.ANY)],
        out_specs=pl.BlockSpec(memory_space=pl.ANY),
        scratch_shapes=[
            pltpu.SemaphoreType.DMA((shards,)),
            pltpu.SemaphoreType.DMA((shards,)),
            pltpu.SemaphoreType.DMA(()),
        ],
        compiler_params=pltpu.CompilerParams(collective_id=collective_id, has_side_effects=True),
    )(x)


def long_conv(pieces):
    blocks, _, group, rows = pieces.shape
    coarse = 2 * blocks
    total = coarse * rows
    half = blocks + 1
    cos1, sin1 = phase_table(half, blocks, coarse, -1.0)
    y_re = jnp.einsum("kd,dsgr->skgr", cos1, pieces, precision=PRECISION)
    y_im = jnp.einsum("kd,dsgr->skgr", sin1, pieces, precision=PRECISION)
    tw_cos, tw_sin = phase_table(half, rows, total, -1.0)
    tw_cos = tw_cos[None, :, None, :]
    tw_sin = tw_sin[None, :, None, :]
    y_re, y_im = y_re * tw_cos - y_im * tw_sin, y_re * tw_sin + y_im * tw_cos
    cos2, sin2 = phase_table(rows, rows, rows, -1.0)
    z_re = jnp.einsum("skgr,rm->skgm", y_re, cos2, precision=PRECISION) - jnp.einsum(
        "skgr,rm->skgm", y_im, sin2, precision=PRECISION
    )
    z_im = jnp.einsum("skgr,rm->skgm", y_im, cos2, precision=PRECISION) + jnp.einsum(
        "skgr,rm->skgm", y_re, sin2, precision=PRECISION
    )
    p_re = z_re[0] * z_re[1] - z_im[0] * z_im[1]
    p_im = z_re[0] * z_im[1] + z_im[0] * z_re[1]
    q_re = jnp.einsum("kgm,mr->kgr", p_re, cos2, precision=PRECISION) + jnp.einsum(
        "kgm,mr->kgr", p_im, sin2, precision=PRECISION
    )
    q_im = jnp.einsum("kgm,mr->kgr", p_im, cos2, precision=PRECISION) - jnp.einsum(
        "kgm,mr->kgr", p_re, sin2, precision=PRECISION
    )
    tw_cos = tw_cos[0]
    tw_sin = tw_sin[0]
    q_re, q_im = q_re * tw_cos + q_im * tw_sin, q_im * tw_cos - q_re * tw_sin
    weight = jnp.where(
        (jnp.arange(half) == 0) | (jnp.arange(half) == blocks), 1.0, 2.0
    ).astype(jnp.float32) / total
    cos3, sin3 = phase_table(blocks, half, coarse, 1.0)
    cos3 = cos3 * weight[None, :]
    sin3 = sin3 * weight[None, :]
    return jnp.einsum("dk,kgr->dgr", cos3, q_re, precision=PRECISION) - jnp.einsum(
        "dk,kgr->dgr", sin3, q_im, precision=PRECISION
    )


def on_device(qkv, short_w, skip, filt):
    rows, _, width = qkv.shape
    taps = short_w.shape[0]
    shards = lax.axis_size("seq")
    group = width // shards
    rim = shifted(qkv[rows - (taps - 1) :], "seq", 1)
    extended = jnp.concatenate([rim, qkv], axis=0).astype(jnp.float32)
    feat = short_w[0] * extended[taps - 1 : taps - 1 + rows]
    for tap in range(1, taps):
        feat = feat + short_w[tap] * extended[taps - 1 - tap : taps - 1 - tap + rows]
    query = feat[:, 0, :]
    signal = feat[:, 1, :] * feat[:, 2, :]
    source = jnp.stack([signal, filt]).reshape(2, rows, shards, group).transpose(2, 0, 3, 1)
    pieces = exchange(source, 0)
    values = long_conv(pieces)
    back = exchange(values, 1)
    conv = back.reshape(width, rows).T
    return (query * (conv + skip * signal)).astype(jnp.bfloat16)


def solution(mesh):
    return jax.shard_map(
        on_device,
        mesh=mesh,
        in_specs=(P("seq", None, "ch"), P(None, None, "ch"), P("ch"), P("seq", "ch")),
        out_specs=P("seq", "ch"),
        check_vma=False,
    )
```

```python
import functools
import math

import jax
import jax.numpy as jnp
from jax import lax
from jax.experimental import pallas as pl
from jax.experimental.pallas import tpu as pltpu
from jax.sharding import PartitionSpec as P

PRECISION = lax.Precision.HIGHEST


def phase_table(count_out, count_in, modulus, sign):
    out_idx = jnp.arange(count_out, dtype=jnp.int32)[:, None]
    in_idx = jnp.arange(count_in, dtype=jnp.int32)[None, :]
    phase = out_idx * in_idx % modulus
    angles = sign * 2.0 * math.pi / modulus * phase.astype(jnp.float32)
    return jnp.cos(angles), jnp.sin(angles)


def exchange_kernel(shards, *refs):
    count = (len(refs) - 2) // 2
    x_refs, o_refs = refs[:count], refs[count : 2 * count]
    send_sem, recv_sem = refs[2 * count :]
    me = lax.axis_index("seq")
    row = lax.axis_index("ch")
    mesh_id = pl.DeviceIdType.MESH
    barrier = pltpu.get_barrier_semaphore()

    def peer_of(step):
        return lax.rem(me + 1 + step, shards)

    def greet(step, carry):
        pl.semaphore_signal(barrier, inc=1, device_id=(peer_of(step), row), device_id_type=mesh_id)
        return carry

    lax.fori_loop(0, shards - 1, greet, 0)
    pl.semaphore_wait(barrier, shards - 1)
    own = [
        pltpu.make_async_copy(x.at[me], o.at[me], send_sem.at[k, me])
        for k, (x, o) in enumerate(zip(x_refs, o_refs))
    ]
    for copy in own:
        copy.start()

    def copy_to(k, peer, slot):
        return pltpu.make_async_remote_copy(
            src_ref=x_refs[k].at[peer],
            dst_ref=o_refs[k].at[slot],
            send_sem=send_sem.at[k, peer],
            recv_sem=recv_sem.at[k, slot],
            device_id=(peer, row),
            device_id_type=mesh_id,
        )

    def send(step, carry):
        peer = peer_of(step)
        for k in range(count):
            copy_to(k, peer, me).start()
        return carry

    lax.fori_loop(0, shards - 1, send, 0)

    def finish(step, carry):
        peer = peer_of(step)
        for k in range(count):
            copy_to(k, peer, me).wait_send()
            copy_to(k, peer, peer).wait_recv()
        return carry

    lax.fori_loop(0, shards - 1, finish, 0)
    for copy in own:
        copy.wait()


def exchange(xs, collective_id):
    shards = xs[0].shape[0]
    count = len(xs)
    return pl.pallas_call(
        functools.partial(exchange_kernel, shards),
        out_shape=[jax.ShapeDtypeStruct(x.shape, x.dtype) for x in xs],
        in_specs=[pl.BlockSpec(memory_space=pl.ANY)] * count,
        out_specs=[pl.BlockSpec(memory_space=pl.ANY)] * count,
        scratch_shapes=[
            pltpu.SemaphoreType.DMA((count, shards)),
            pltpu.SemaphoreType.DMA((count, shards)),
        ],
        compiler_params=pltpu.CompilerParams(collective_id=collective_id, has_side_effects=True),
    )(*xs)


def long_conv(pieces):
    blocks, _, group, rows = pieces.shape
    coarse = 2 * blocks
    total = coarse * rows
    half = blocks + 1
    cos1, sin1 = phase_table(half, blocks, coarse, -1.0)
    y_re = jnp.einsum("kd,dsgr->skgr", cos1, pieces, precision=PRECISION)
    y_im = jnp.einsum("kd,dsgr->skgr", sin1, pieces, precision=PRECISION)
    tw_cos, tw_sin = phase_table(half, rows, total, -1.0)
    tw_cos = tw_cos[None, :, None, :]
    tw_sin = tw_sin[None, :, None, :]
    y_re, y_im = y_re * tw_cos - y_im * tw_sin, y_re * tw_sin + y_im * tw_cos
    cos2, sin2 = phase_table(rows, rows, rows, -1.0)
    z_re = jnp.einsum("skgr,rm->skgm", y_re, cos2, precision=PRECISION) - jnp.einsum(
        "skgr,rm->skgm", y_im, sin2, precision=PRECISION
    )
    z_im = jnp.einsum("skgr,rm->skgm", y_im, cos2, precision=PRECISION) + jnp.einsum(
        "skgr,rm->skgm", y_re, sin2, precision=PRECISION
    )
    p_re = z_re[0] * z_re[1] - z_im[0] * z_im[1]
    p_im = z_re[0] * z_im[1] + z_im[0] * z_re[1]
    q_re = jnp.einsum("kgm,mr->kgr", p_re, cos2, precision=PRECISION) + jnp.einsum(
        "kgm,mr->kgr", p_im, sin2, precision=PRECISION
    )
    q_im = jnp.einsum("kgm,mr->kgr", p_im, cos2, precision=PRECISION) - jnp.einsum(
        "kgm,mr->kgr", p_re, sin2, precision=PRECISION
    )
    tw_cos = tw_cos[0]
    tw_sin = tw_sin[0]
    q_re, q_im = q_re * tw_cos + q_im * tw_sin, q_im * tw_cos - q_re * tw_sin
    weight = jnp.where(
        (jnp.arange(half) == 0) | (jnp.arange(half) == blocks), 1.0, 2.0
    ).astype(jnp.float32) / total
    cos3, sin3 = phase_table(blocks, half, coarse, 1.0)
    cos3 = cos3 * weight[None, :]
    sin3 = sin3 * weight[None, :]
    return jnp.einsum("dk,kgr->dgr", cos3, q_re, precision=PRECISION) - jnp.einsum(
        "dk,kgr->dgr", sin3, q_im, precision=PRECISION
    )


def on_device(qkv, short_w, skip, filt):
    rows, streams, width = qkv.shape
    taps = short_w.shape[0]
    shards = lax.axis_size("seq")
    group = width // shards
    place = lax.axis_index("seq")
    qkv_out = qkv.reshape(rows, streams, shards, group).transpose(2, 1, 3, 0)
    filt_out = filt.reshape(rows, shards, group).transpose(1, 2, 0)
    qkv_in, filt_in = exchange([qkv_out, filt_out], 0)
    length = shards * rows
    wide = qkv_in.astype(jnp.float32).transpose(1, 2, 0, 3).reshape(streams, group, length)
    extended = jnp.pad(wide, ((0, 0), (0, 0), (taps - 1, 0)))
    weights = lax.dynamic_slice_in_dim(short_w, place * group, group, axis=2)[:, :, :, None]
    feat = weights[0] * extended[:, :, taps - 1 : taps - 1 + length]
    for tap in range(1, taps):
        feat = feat + weights[tap] * extended[:, :, taps - 1 - tap : taps - 1 - tap + length]
    feat = feat.reshape(streams, group, shards, rows).transpose(0, 2, 1, 3)
    query = feat[0]
    signal = feat[1] * feat[2]
    conv = long_conv(jnp.stack([signal, filt_in], axis=1))
    gain = lax.dynamic_slice_in_dim(skip, place * group, group)[None, :, None]
    mixed = (query * (conv + gain * signal)).astype(jnp.bfloat16)
    (back,) = exchange([mixed], 1)
    return back.reshape(width, rows).T


def solution(mesh):
    return jax.shard_map(
        on_device,
        mesh=mesh,
        in_specs=(P("seq", None, "ch"), P(None, None, "ch"), P("ch"), P("seq", "ch")),
        out_specs=P("seq", "ch"),
        check_vma=False,
    )
```

```python
import functools
import math

import jax
import jax.numpy as jnp
from jax import lax
from jax.experimental import pallas as pl
from jax.experimental.pallas import tpu as pltpu
from jax.sharding import PartitionSpec as P

PRECISION = lax.Precision.HIGHEST


def phase_table(count_out, count_in, modulus, sign):
    out_idx = jnp.arange(count_out, dtype=jnp.int32)[:, None]
    in_idx = jnp.arange(count_in, dtype=jnp.int32)[None, :]
    phase = out_idx * in_idx % modulus
    angles = sign * 2.0 * math.pi / modulus * phase.astype(jnp.float32)
    return jnp.cos(angles), jnp.sin(angles)


def exchange_kernel(shards, *refs):
    count = (len(refs) - 2) // 2
    x_refs, o_refs = refs[:count], refs[count : 2 * count]
    send_sem, recv_sem = refs[2 * count :]
    me = lax.axis_index("seq")
    row = lax.axis_index("ch")
    mesh_id = pl.DeviceIdType.MESH
    barrier = pltpu.get_barrier_semaphore()

    def peer_of(step):
        return lax.rem(me + 1 + step, shards)

    def greet(step, carry):
        pl.semaphore_signal(barrier, inc=1, device_id=(peer_of(step), row), device_id_type=mesh_id)
        return carry

    lax.fori_loop(0, shards - 1, greet, 0)
    pl.semaphore_wait(barrier, shards - 1)
    own = [
        pltpu.make_async_copy(x.at[me], o.at[me], send_sem.at[k, me])
        for k, (x, o) in enumerate(zip(x_refs, o_refs))
    ]
    for copy in own:
        copy.start()

    def copy_to(k, peer, slot):
        return pltpu.make_async_remote_copy(
            src_ref=x_refs[k].at[peer],
            dst_ref=o_refs[k].at[slot],
            send_sem=send_sem.at[k, peer],
            recv_sem=recv_sem.at[k, slot],
            device_id=(peer, row),
            device_id_type=mesh_id,
        )

    def send(step, carry):
        peer = peer_of(step)
        for k in range(count):
            copy_to(k, peer, me).start()
        return carry

    lax.fori_loop(0, shards - 1, send, 0)

    def finish(step, carry):
        peer = peer_of(step)
        for k in range(count):
            copy_to(k, peer, me).wait_send()
            copy_to(k, peer, peer).wait_recv()
        return carry

    lax.fori_loop(0, shards - 1, finish, 0)
    for copy in own:
        copy.wait()


def exchange(xs, collective_id):
    shards = xs[0].shape[0]
    count = len(xs)
    return pl.pallas_call(
        functools.partial(exchange_kernel, shards),
        out_shape=[jax.ShapeDtypeStruct(x.shape, x.dtype) for x in xs],
        in_specs=[pl.BlockSpec(memory_space=pl.ANY)] * count,
        out_specs=[pl.BlockSpec(memory_space=pl.ANY)] * count,
        scratch_shapes=[
            pltpu.SemaphoreType.DMA((count, shards)),
            pltpu.SemaphoreType.DMA((count, shards)),
        ],
        compiler_params=pltpu.CompilerParams(collective_id=collective_id, has_side_effects=True),
    )(*xs)


def conv_kernel(
    x_ref, c1_ref, s1_ref, twc_ref, tws_ref, vc_ref, vs_ref, ci_ref, si_ref, o_ref, yre_ref, yim_ref
):
    streams = x_ref.shape[0]
    group = streams // 2
    pad = c1_ref.shape[0]

    def dot(a, b):
        return jnp.dot(a, b, precision=PRECISION, preferred_element_type=jnp.float32)

    twc = twc_ref[...]
    tws = tws_ref[...]
    c1 = c1_ref[...]
    s1 = s1_ref[...]
    for j in range(streams):
        xj = x_ref[j]
        a = dot(c1, xj)
        b = dot(s1, xj)
        yre_ref[j * pad : (j + 1) * pad, :] = a * twc - b * tws
        yim_ref[j * pad : (j + 1) * pad, :] = a * tws + b * twc
    vc = vc_ref[...]
    vs = vs_ref[...]
    yre = yre_ref[...]
    yim = yim_ref[...]
    zre = dot(yre, vc) - dot(yim, vs)
    zim = dot(yim, vc) + dot(yre, vs)
    half = group * pad
    pre = zre[:half] * zre[half:] - zim[:half] * zim[half:]
    pim = zre[:half] * zim[half:] + zim[:half] * zre[half:]
    qre = dot(pre, vc) + dot(pim, vs)
    qim = dot(pim, vc) - dot(pre, vs)
    ci = ci_ref[...]
    si = si_ref[...]
    for g in range(group):
        ure = qre[g * pad : (g + 1) * pad]
        uim = qim[g * pad : (g + 1) * pad]
        vre = ure * twc + uim * tws
        vim = uim * twc - ure * tws
        o_ref[g] = dot(ci, vre) - dot(si, vim)


def long_conv(pieces):
    streams, blocks, rows = pieces.shape
    group = streams // 2
    coarse = 2 * blocks
    total = coarse * rows
    half = blocks + 1
    pad = -(-half // 8) * 8
    live = (jnp.arange(pad) < half).astype(jnp.float32)
    c1, s1 = phase_table(pad, blocks, coarse, -1.0)
    c1 = c1 * live[:, None]
    s1 = s1 * live[:, None]
    twc, tws = phase_table(pad, rows, total, -1.0)
    vc, vs = phase_table(rows, rows, rows, -1.0)
    k1 = jnp.arange(pad)
    weight = jnp.where((k1 == 0) | (k1 == blocks), 1.0, 2.0) * live / total
    ci, si = phase_table(blocks, pad, coarse, 1.0)
    ci = ci * weight[None, :]
    si = si * weight[None, :]
    vmem = pl.BlockSpec(memory_space=pltpu.VMEM)
    return pl.pallas_call(
        conv_kernel,
        out_shape=jax.ShapeDtypeStruct((group, blocks, rows), jnp.float32),
        in_specs=[vmem] * 9,
        out_specs=vmem,
        scratch_shapes=[
            pltpu.VMEM((streams * pad, rows), jnp.float32),
            pltpu.VMEM((streams * pad, rows), jnp.float32),
        ],
    )(pieces, c1, s1, twc, tws, vc, vs, ci, si)


def on_device(qkv, short_w, skip, filt):
    rows, streams, width = qkv.shape
    taps = short_w.shape[0]
    shards = lax.axis_size("seq")
    group = width // shards
    place = lax.axis_index("seq")
    qkv_out = qkv.reshape(rows, streams, shards, group).transpose(2, 1, 3, 0)
    filt_out = filt.reshape(rows, shards, group).transpose(1, 2, 0)
    qkv_in, filt_in = exchange([qkv_out, filt_out], 0)
    length = shards * rows
    wide = qkv_in.astype(jnp.float32).transpose(1, 2, 0, 3).reshape(streams, group, length)
    extended = jnp.pad(wide, ((0, 0), (0, 0), (taps - 1, 0)))
    weights = lax.dynamic_slice_in_dim(short_w, place * group, group, axis=2)[:, :, :, None]
    feat = weights[0] * extended[:, :, taps - 1 : taps - 1 + length]
    for tap in range(1, taps):
        feat = feat + weights[tap] * extended[:, :, taps - 1 - tap : taps - 1 - tap + length]
    feat = feat.reshape(streams, group, shards, rows).transpose(0, 2, 1, 3)
    query = feat[0]
    signal = feat[1] * feat[2]
    pieces = jnp.concatenate([signal, filt_in], axis=1).transpose(1, 0, 2)
    conv = long_conv(pieces).transpose(1, 0, 2)
    gain = lax.dynamic_slice_in_dim(skip, place * group, group)[None, :, None]
    mixed = (query * (conv + gain * signal)).astype(jnp.bfloat16)
    (back,) = exchange([mixed], 1)
    return back.reshape(width, rows).T


def solution(mesh):
    return jax.shard_map(
        on_device,
        mesh=mesh,
        in_specs=(P("seq", None, "ch"), P(None, None, "ch"), P("ch"), P("seq", "ch")),
        out_specs=P("seq", "ch"),
        check_vma=False,
    )
```

```python
import functools
import math

import jax
import numpy as np
import jax.numpy as jnp
from jax import lax
from jax.experimental import pallas as pl
from jax.experimental.pallas import tpu as pltpu
from jax.sharding import PartitionSpec as P

PRECISION = lax.Precision.HIGHEST


def phase_table(count_out, count_in, modulus, sign):
    phase = np.arange(count_out)[:, None] * np.arange(count_in)[None, :] % modulus
    angles = sign * 2.0 * np.pi / modulus * phase
    return np.cos(angles), np.sin(angles)


def exchange_kernel(shards, *refs):
    count = (len(refs) - 2) // 2
    x_refs, o_refs = refs[:count], refs[count : 2 * count]
    send_sem, recv_sem = refs[2 * count :]
    me = lax.axis_index("seq")
    row = lax.axis_index("ch")
    mesh_id = pl.DeviceIdType.MESH
    barrier = pltpu.get_barrier_semaphore()

    def peer_of(step):
        return lax.rem(me + 1 + step, shards)

    def greet(step, carry):
        pl.semaphore_signal(barrier, inc=1, device_id=(peer_of(step), row), device_id_type=mesh_id)
        return carry

    lax.fori_loop(0, shards - 1, greet, 0)
    pl.semaphore_wait(barrier, shards - 1)
    own = [
        pltpu.make_async_copy(x.at[me], o.at[me], send_sem.at[k, me])
        for k, (x, o) in enumerate(zip(x_refs, o_refs))
    ]
    for copy in own:
        copy.start()

    def copy_to(k, peer, slot):
        return pltpu.make_async_remote_copy(
            src_ref=x_refs[k].at[peer],
            dst_ref=o_refs[k].at[slot],
            send_sem=send_sem.at[k, peer],
            recv_sem=recv_sem.at[k, slot],
            device_id=(peer, row),
            device_id_type=mesh_id,
        )

    def send(step, carry):
        peer = peer_of(step)
        for k in range(count):
            copy_to(k, peer, me).start()
        return carry

    lax.fori_loop(0, shards - 1, send, 0)

    def finish(step, carry):
        peer = peer_of(step)
        for k in range(count):
            copy_to(k, peer, me).wait_send()
            copy_to(k, peer, peer).wait_recv()
        return carry

    lax.fori_loop(0, shards - 1, finish, 0)
    for copy in own:
        copy.wait()


def exchange(xs, collective_id):
    shards = xs[0].shape[0]
    count = len(xs)
    return pl.pallas_call(
        functools.partial(exchange_kernel, shards),
        out_shape=[jax.ShapeDtypeStruct(x.shape, x.dtype) for x in xs],
        in_specs=[pl.BlockSpec(memory_space=pl.ANY)] * count,
        out_specs=[pl.BlockSpec(memory_space=pl.ANY)] * count,
        scratch_shapes=[
            pltpu.SemaphoreType.DMA((count, shards)),
            pltpu.SemaphoreType.DMA((count, shards)),
        ],
        compiler_params=pltpu.CompilerParams(collective_id=collective_id, has_side_effects=True),
    )(*xs)


def conv_kernel(
    x_ref, c1_ref, s1_ref, twc_ref, tws_ref, vc_ref, vs_ref, vsum_ref, vdiff_ref, ci_ref, si_ref, o_ref,
    yre_ref, yim_ref,
):
    streams = x_ref.shape[0]
    group = streams // 2
    pad = c1_ref.shape[0]

    def dot(a, b):
        return jnp.dot(a, b, precision=PRECISION, preferred_element_type=jnp.float32)

    twc = twc_ref[...]
    tws = tws_ref[...]
    c1 = c1_ref[...]
    s1 = s1_ref[...]
    for j in range(streams):
        xj = x_ref[j]
        a = dot(c1, xj)
        b = dot(s1, xj)
        yre_ref[j * pad : (j + 1) * pad, :] = a * twc - b * tws
        yim_ref[j * pad : (j + 1) * pad, :] = a * tws + b * twc
    vc = vc_ref[...]
    vs = vs_ref[...]
    yre = yre_ref[...]
    yim = yim_ref[...]
    vsum = vsum_ref[...]
    ac = dot(yre, vc)
    bd = dot(yim, vs)
    zre = ac - bd
    zim = dot(yre + yim, vsum) - ac - bd
    half = group * pad
    pre = zre[:half] * zre[half:] - zim[:half] * zim[half:]
    pim = zre[:half] * zim[half:] + zim[:half] * zre[half:]
    vdiff = vdiff_ref[...]
    ac = dot(pre, vc)
    bd = dot(pim, vs)
    qre = ac + bd
    qim = dot(pre + pim, vdiff) - ac + bd
    ci = ci_ref[...]
    si = si_ref[...]
    for g in range(group):
        ure = qre[g * pad : (g + 1) * pad]
        uim = qim[g * pad : (g + 1) * pad]
        vre = ure * twc + uim * tws
        vim = uim * twc - ure * tws
        o_ref[g] = dot(ci, vre) - dot(si, vim)


def long_conv(pieces):
    streams, blocks, rows = pieces.shape
    group = streams // 2
    coarse = 2 * blocks
    total = coarse * rows
    half = blocks + 1
    pad = -(-half // 8) * 8
    live = (np.arange(pad) < half).astype(np.float64)
    c1, s1 = phase_table(pad, blocks, coarse, -1.0)
    c1 = c1 * live[:, None]
    s1 = s1 * live[:, None]
    twc, tws = phase_table(pad, rows, total, -1.0)
    vc, vs = phase_table(rows, rows, rows, -1.0)
    k1 = np.arange(pad)
    weight = np.where((k1 == 0) | (k1 == blocks), 1.0, 2.0) * live / total
    ci, si = phase_table(blocks, pad, coarse, 1.0)
    ci = ci * weight[None, :]
    si = si * weight[None, :]
    tables = [c1, s1, twc, tws, vc, vs, vc + vs, vc - vs, ci, si]
    tables = [jnp.asarray(t, dtype=jnp.float32) for t in tables]
    vmem = pl.BlockSpec(memory_space=pltpu.VMEM)
    return pl.pallas_call(
        conv_kernel,
        out_shape=jax.ShapeDtypeStruct((group, blocks, rows), jnp.float32),
        in_specs=[vmem] * (1 + len(tables)),
        out_specs=vmem,
        scratch_shapes=[
            pltpu.VMEM((streams * pad, rows), jnp.float32),
            pltpu.VMEM((streams * pad, rows), jnp.float32),
        ],
    )(pieces, *tables)


def on_device(qkv, short_w, skip, filt):
    rows, streams, width = qkv.shape
    taps = short_w.shape[0]
    shards = lax.axis_size("seq")
    group = width // shards
    place = lax.axis_index("seq")
    qkv_out = qkv.reshape(rows, streams, shards, group).transpose(2, 1, 3, 0)
    filt_out = filt.reshape(rows, shards, group).transpose(1, 2, 0)
    qkv_in, filt_in = exchange([qkv_out, filt_out], 0)
    length = shards * rows
    wide = qkv_in.astype(jnp.float32).transpose(1, 2, 0, 3).reshape(streams, group, length)
    extended = jnp.pad(wide, ((0, 0), (0, 0), (taps - 1, 0)))
    weights = lax.dynamic_slice_in_dim(short_w, place * group, group, axis=2)[:, :, :, None]
    feat = weights[0] * extended[:, :, taps - 1 : taps - 1 + length]
    for tap in range(1, taps):
        feat = feat + weights[tap] * extended[:, :, taps - 1 - tap : taps - 1 - tap + length]
    feat = feat.reshape(streams, group, shards, rows).transpose(0, 2, 1, 3)
    query = feat[0]
    signal = feat[1] * feat[2]
    pieces = jnp.concatenate([signal, filt_in], axis=1).transpose(1, 0, 2)
    conv = long_conv(pieces).transpose(1, 0, 2)
    gain = lax.dynamic_slice_in_dim(skip, place * group, group)[None, :, None]
    mixed = (query * (conv + gain * signal)).astype(jnp.bfloat16)
    (back,) = exchange([mixed], 1)
    return back.reshape(width, rows).T


def solution(mesh):
    return jax.shard_map(
        on_device,
        mesh=mesh,
        in_specs=(P("seq", None, "ch"), P(None, None, "ch"), P("ch"), P("seq", "ch")),
        out_specs=P("seq", "ch"),
        check_vma=False,
    )
```

```python
import functools
import math

import jax
import numpy as np
import jax.numpy as jnp
from jax import lax
from jax.experimental import pallas as pl
from jax.experimental.pallas import tpu as pltpu
from jax.sharding import PartitionSpec as P

PRECISION = lax.Precision.HIGHEST


def phase_table(count_out, count_in, modulus, sign):
    phase = np.arange(count_out)[:, None] * np.arange(count_in)[None, :] % modulus
    angles = sign * 2.0 * np.pi / modulus * phase
    return np.cos(angles), np.sin(angles)


def conv_body(
    x_ref, c1_ref, s1_ref, twc_ref, tws_ref, vc_ref, vs_ref, vsum_ref, vdiff_ref, ci_ref, si_ref, o_ref,
    yre_ref, yim_ref,
):
    streams = x_ref.shape[0]
    group = streams // 2
    pad = c1_ref.shape[0]

    def dot(a, b):
        return jnp.dot(a, b, precision=PRECISION, preferred_element_type=jnp.float32)

    twc = twc_ref[...]
    tws = tws_ref[...]
    c1 = c1_ref[...]
    s1 = s1_ref[...]
    for j in range(streams):
        xj = x_ref[j]
        a = dot(c1, xj)
        b = dot(s1, xj)
        yre_ref[j * pad : (j + 1) * pad, :] = a * twc - b * tws
        yim_ref[j * pad : (j + 1) * pad, :] = a * tws + b * twc
    vc = vc_ref[...]
    vs = vs_ref[...]
    yre = yre_ref[...]
    yim = yim_ref[...]
    vsum = vsum_ref[...]
    ac = dot(yre, vc)
    bd = dot(yim, vs)
    zre = ac - bd
    zim = dot(yre + yim, vsum) - ac - bd
    half = group * pad
    pre = zre[:half] * zre[half:] - zim[:half] * zim[half:]
    pim = zre[:half] * zim[half:] + zim[:half] * zre[half:]
    vdiff = vdiff_ref[...]
    ac = dot(pre, vc)
    bd = dot(pim, vs)
    qre = ac + bd
    qim = dot(pre + pim, vdiff) - ac + bd
    ci = ci_ref[...]
    si = si_ref[...]
    for g in range(group):
        ure = qre[g * pad : (g + 1) * pad]
        uim = qim[g * pad : (g + 1) * pad]
        vre = ure * twc + uim * tws
        vim = uim * twc - ure * tws
        o_ref[g] = dot(ci, vre) - dot(si, vim)


def fused_kernel(shards, src_ref, *refs):
    tables = refs[:10]
    out_ref, recv_ref, stage_ref = refs[10:13]
    x_ref, o_ref, yre_ref, yim_ref, send_a, recv_a, send_b, recv_b, local = refs[13:]
    me = lax.axis_index("seq")
    row = lax.axis_index("ch")
    mesh_id = pl.DeviceIdType.MESH
    streams = x_ref.shape[0]
    barrier = pltpu.get_barrier_semaphore()

    def peer_of(step):
        return lax.rem(me + 1 + step, shards)

    def greet(step, carry):
        pl.semaphore_signal(barrier, inc=1, device_id=(peer_of(step), row), device_id_type=mesh_id)
        return carry

    lax.fori_loop(0, shards - 1, greet, 0)
    pl.semaphore_wait(barrier, shards - 1)

    def scatter(source, target, send_sem, recv_sem, own_sem):
        own = pltpu.make_async_copy(source(me), target.at[me], own_sem)
        own.start()

        def copy_to(peer, slot):
            return pltpu.make_async_remote_copy(
                src_ref=source(peer),
                dst_ref=target.at[slot],
                send_sem=send_sem.at[peer],
                recv_sem=recv_sem.at[slot],
                device_id=(peer, row),
                device_id_type=mesh_id,
            )

        def send(step, carry):
            copy_to(peer_of(step), me).start()
            return carry

        def finish(step, carry):
            peer = peer_of(step)
            copy_to(peer, me).wait_send()
            copy_to(peer, peer).wait_recv()
            return carry

        lax.fori_loop(0, shards - 1, send, 0)
        lax.fori_loop(0, shards - 1, finish, 0)
        own.wait()

    scatter(lambda j: src_ref.at[j], recv_ref, send_a, recv_a, local.at[0])
    gathers = [
        pltpu.make_async_copy(recv_ref.at[:, j, :], x_ref.at[j], local.at[2 + j])
        for j in range(streams)
    ]
    for copy in gathers:
        copy.start()
    for copy in gathers:
        copy.wait()
    conv_body(x_ref, *tables, o_ref, yre_ref, yim_ref)
    put = pltpu.make_async_copy(o_ref, stage_ref, local.at[1])
    put.start()
    put.wait()
    scatter(lambda j: stage_ref.at[:, j, :], out_ref, send_b, recv_b, local.at[0])


def long_conv(pieces):
    blocks, streams, rows = pieces.shape
    group = streams // 2
    coarse = 2 * blocks
    total = coarse * rows
    half = blocks + 1
    pad = -(-half // 8) * 8
    live = (np.arange(pad) < half).astype(np.float64)
    c1, s1 = phase_table(pad, blocks, coarse, -1.0)
    c1 = c1 * live[:, None]
    s1 = s1 * live[:, None]
    twc, tws = phase_table(pad, rows, total, -1.0)
    vc, vs = phase_table(rows, rows, rows, -1.0)
    k1 = np.arange(pad)
    weight = np.where((k1 == 0) | (k1 == blocks), 1.0, 2.0) * live / total
    ci, si = phase_table(blocks, pad, coarse, 1.0)
    ci = ci * weight[None, :]
    si = si * weight[None, :]
    tables = [c1, s1, twc, tws, vc, vs, vc + vs, vc - vs, ci, si]
    tables = [jnp.asarray(t, dtype=jnp.float32) for t in tables]
    vmem = pl.BlockSpec(memory_space=pltpu.VMEM)
    anywhere = pl.BlockSpec(memory_space=pl.ANY)
    f32 = jnp.float32
    return pl.pallas_call(
        functools.partial(fused_kernel, blocks),
        out_shape=[
            jax.ShapeDtypeStruct((blocks, group, rows), f32),
            jax.ShapeDtypeStruct((blocks, streams, rows), f32),
            jax.ShapeDtypeStruct((group, blocks, rows), f32),
        ],
        in_specs=[anywhere] + [vmem] * len(tables),
        out_specs=[anywhere] * 3,
        scratch_shapes=[
            pltpu.VMEM((streams, blocks, rows), f32),
            pltpu.VMEM((group, blocks, rows), f32),
            pltpu.VMEM((streams * pad, rows), f32),
            pltpu.VMEM((streams * pad, rows), f32),
            pltpu.SemaphoreType.DMA((blocks,)),
            pltpu.SemaphoreType.DMA((blocks,)),
            pltpu.SemaphoreType.DMA((blocks,)),
            pltpu.SemaphoreType.DMA((blocks,)),
            pltpu.SemaphoreType.DMA((2 + streams,)),
        ],
        compiler_params=pltpu.CompilerParams(collective_id=0, has_side_effects=True),
    )(pieces, *tables)[0]


def shifted(block, axis, distance):
    devices = range(lax.axis_size(axis))
    route = [(i - distance, i) for i in devices if i - distance in devices]
    return lax.ppermute(block, axis, route)


def on_device(qkv, short_w, skip, filt):
    rows, _, width = qkv.shape
    taps = short_w.shape[0]
    shards = lax.axis_size("seq")
    group = width // shards
    rim = shifted(qkv[rows - (taps - 1) :], "seq", 1)
    extended = jnp.concatenate([rim, qkv], axis=0).astype(jnp.float32)
    feat = short_w[0] * extended[taps - 1 : taps - 1 + rows]
    for tap in range(1, taps):
        feat = feat + short_w[tap] * extended[taps - 1 - tap : taps - 1 - tap + rows]
    query = feat[:, 0, :]
    signal = feat[:, 1, :] * feat[:, 2, :]
    source = jnp.stack([signal, filt]).reshape(2, rows, shards, group).transpose(2, 0, 3, 1)
    values = long_conv(source.reshape(shards, 2 * group, rows))
    conv = values.reshape(width, rows).T
    return (query * (conv + skip * signal)).astype(jnp.bfloat16)


def solution(mesh):
    return jax.shard_map(
        on_device,
        mesh=mesh,
        in_specs=(P("seq", None, "ch"), P(None, None, "ch"), P("ch"), P("seq", "ch")),
        out_specs=P("seq", "ch"),
        check_vma=False,
    )
```

```python
import functools
import math

import jax
import numpy as np
import jax.numpy as jnp
from jax import lax
from jax.experimental import pallas as pl
from jax.experimental.pallas import tpu as pltpu
from jax.sharding import PartitionSpec as P

PRECISION = lax.Precision.HIGHEST


def phase_table(count_out, count_in, modulus, sign):
    phase = np.arange(count_out)[:, None] * np.arange(count_in)[None, :] % modulus
    angles = sign * 2.0 * np.pi / modulus * phase
    return np.cos(angles), np.sin(angles)


def conv_body(
    x_ref, c1_ref, s1_ref, twc_ref, tws_ref, vc_ref, vs_ref, vsum_ref, vdiff_ref, ci_ref, si_ref, o_ref,
    yre_ref, yim_ref,
):
    streams = x_ref.shape[0]
    group = streams // 2
    pad = c1_ref.shape[0]

    def dot(a, b):
        return jnp.dot(a, b, precision=PRECISION, preferred_element_type=jnp.float32)

    twc = twc_ref[...]
    tws = tws_ref[...]
    c1 = c1_ref[...]
    s1 = s1_ref[...]
    for j in range(streams):
        xj = x_ref[j]
        a = dot(c1, xj)
        b = dot(s1, xj)
        yre_ref[j * pad : (j + 1) * pad, :] = a * twc - b * tws
        yim_ref[j * pad : (j + 1) * pad, :] = a * tws + b * twc
    vc = vc_ref[...]
    vs = vs_ref[...]
    yre = yre_ref[...]
    yim = yim_ref[...]
    vsum = vsum_ref[...]
    ac = dot(yre, vc)
    bd = dot(yim, vs)
    zre = ac - bd
    zim = dot(yre + yim, vsum) - ac - bd
    half = group * pad
    pre = zre[:half] * zre[half:] - zim[:half] * zim[half:]
    pim = zre[:half] * zim[half:] + zim[:half] * zre[half:]
    vdiff = vdiff_ref[...]
    ac = dot(pre, vc)
    bd = dot(pim, vs)
    qre = ac + bd
    qim = dot(pre + pim, vdiff) - ac + bd
    ci = ci_ref[...]
    si = si_ref[...]
    for g in range(group):
        ure = qre[g * pad : (g + 1) * pad]
        uim = qim[g * pad : (g + 1) * pad]
        vre = ure * twc + uim * tws
        vim = uim * twc - ure * tws
        o_ref[g] = dot(ci, vre) - dot(si, vim)


def fused_kernel(shards, parts, src_ref, *refs):
    tables = refs[:10]
    out_ref, recv_ref, stage_ref = refs[10:13]
    x_ref, o_ref, yre_ref, yim_ref, sends, recvs, local = refs[13:]
    me = lax.axis_index("seq")
    row = lax.axis_index("ch")
    mesh_id = pl.DeviceIdType.MESH
    streams = x_ref.shape[0]
    barrier = pltpu.get_barrier_semaphore()

    def peer_of(step):
        return lax.rem(me + 1 + step, shards)

    def greet(step, carry):
        pl.semaphore_signal(barrier, inc=1, device_id=(peer_of(step), row), device_id_type=mesh_id)
        return carry

    lax.fori_loop(0, shards - 1, greet, 0)
    pl.semaphore_wait(barrier, shards - 1)

    def scatter(source, target, phase):
        own = pltpu.make_async_copy(source(me), target(me), local.at[phase])
        own.start()

        def copy_to(peer, slot):
            return pltpu.make_async_remote_copy(
                src_ref=source(peer),
                dst_ref=target(slot),
                send_sem=sends.at[phase, peer],
                recv_sem=recvs.at[phase, slot],
                device_id=(peer, row),
                device_id_type=mesh_id,
            )

        def send(step, carry):
            copy_to(peer_of(step), me).start()
            return carry

        lax.fori_loop(0, shards - 1, send, 0)

        def finish():
            def wait_one(step, carry):
                peer = peer_of(step)
                copy_to(peer, me).wait_send()
                copy_to(peer, peer).wait_recv()
                return carry

            lax.fori_loop(0, shards - 1, wait_one, 0)
            own.wait()

        return finish

    arrivals = [
        scatter(lambda j, h=h: src_ref.at[j, h], lambda j, h=h: recv_ref.at[j, h], h)
        for h in range(parts)
    ]
    returns = []
    for h in range(parts):
        arrivals[h]()
        gathers = [
            pltpu.make_async_copy(recv_ref.at[:, h, j, :], x_ref.at[j], local.at[2 * parts + j])
            for j in range(streams)
        ]
        for copy in gathers:
            copy.start()
        for copy in gathers:
            copy.wait()
        conv_body(x_ref, *tables, o_ref, yre_ref, yim_ref)
        put = pltpu.make_async_copy(o_ref, stage_ref.at[h], local.at[2 * parts + streams])
        put.start()
        put.wait()
        returns.append(
            scatter(
                lambda j, h=h: stage_ref.at[h, :, j, :],
                lambda j, h=h: out_ref.at[j, h],
                parts + h,
            )
        )
    for finish in returns:
        finish()


def long_conv(pieces):
    blocks, parts, streams, rows = pieces.shape
    group = streams // 2
    coarse = 2 * blocks
    total = coarse * rows
    half = blocks + 1
    pad = -(-half // 8) * 8
    live = (np.arange(pad) < half).astype(np.float64)
    c1, s1 = phase_table(pad, blocks, coarse, -1.0)
    c1 = c1 * live[:, None]
    s1 = s1 * live[:, None]
    twc, tws = phase_table(pad, rows, total, -1.0)
    vc, vs = phase_table(rows, rows, rows, -1.0)
    k1 = np.arange(pad)
    weight = np.where((k1 == 0) | (k1 == blocks), 1.0, 2.0) * live / total
    ci, si = phase_table(blocks, pad, coarse, 1.0)
    ci = ci * weight[None, :]
    si = si * weight[None, :]
    tables = [c1, s1, twc, tws, vc, vs, vc + vs, vc - vs, ci, si]
    tables = [jnp.asarray(t, dtype=jnp.float32) for t in tables]
    vmem = pl.BlockSpec(memory_space=pltpu.VMEM)
    anywhere = pl.BlockSpec(memory_space=pl.ANY)
    f32 = jnp.float32
    return pl.pallas_call(
        functools.partial(fused_kernel, blocks, parts),
        out_shape=[
            jax.ShapeDtypeStruct((blocks, parts, group, rows), f32),
            jax.ShapeDtypeStruct((blocks, parts, streams, rows), f32),
            jax.ShapeDtypeStruct((parts, group, blocks, rows), f32),
        ],
        in_specs=[anywhere] + [vmem] * len(tables),
        out_specs=[anywhere] * 3,
        scratch_shapes=[
            pltpu.VMEM((streams, blocks, rows), f32),
            pltpu.VMEM((group, blocks, rows), f32),
            pltpu.VMEM((streams * pad, rows), f32),
            pltpu.VMEM((streams * pad, rows), f32),
            pltpu.SemaphoreType.DMA((2 * parts, blocks)),
            pltpu.SemaphoreType.DMA((2 * parts, blocks)),
            pltpu.SemaphoreType.DMA((2 * parts + streams + 1,)),
        ],
        compiler_params=pltpu.CompilerParams(collective_id=0, has_side_effects=True),
    )(pieces, *tables)[0]


def shifted(block, axis, distance):
    devices = range(lax.axis_size(axis))
    route = [(i - distance, i) for i in devices if i - distance in devices]
    return lax.ppermute(block, axis, route)


def on_device(qkv, short_w, skip, filt):
    rows, _, width = qkv.shape
    taps = short_w.shape[0]
    shards = lax.axis_size("seq")
    group = width // shards
    rim = shifted(qkv[rows - (taps - 1) :], "seq", 1)
    extended = jnp.concatenate([rim, qkv], axis=0).astype(jnp.float32)
    feat = short_w[0] * extended[taps - 1 : taps - 1 + rows]
    for tap in range(1, taps):
        feat = feat + short_w[tap] * extended[taps - 1 - tap : taps - 1 - tap + rows]
    query = feat[:, 0, :]
    signal = feat[:, 1, :] * feat[:, 2, :]
    parts = 2
    source = jnp.stack([signal, filt]).reshape(2, rows, shards, parts, group // parts)
    source = source.transpose(2, 3, 0, 4, 1).reshape(shards, parts, 2 * group // parts, rows)
    values = long_conv(source)
    conv = values.reshape(width, rows).T
    return (query * (conv + skip * signal)).astype(jnp.bfloat16)


def solution(mesh):
    return jax.shard_map(
        on_device,
        mesh=mesh,
        in_specs=(P("seq", None, "ch"), P(None, None, "ch"), P("ch"), P("seq", "ch")),
        out_specs=P("seq", "ch"),
        check_vma=False,
    )
```

```python
import functools
import math

import jax
import numpy as np
import jax.numpy as jnp
from jax import lax
from jax.experimental import pallas as pl
from jax.experimental.pallas import tpu as pltpu
from jax.sharding import PartitionSpec as P

PRECISION = lax.Precision.HIGHEST


def phase_table(count_out, count_in, modulus, sign):
    phase = np.arange(count_out)[:, None] * np.arange(count_in)[None, :] % modulus
    angles = sign * 2.0 * np.pi / modulus * phase
    return np.cos(angles), np.sin(angles)


def conv_body(
    x_ref, c1_ref, s1_ref, twc_ref, tws_ref, vc_ref, vs_ref, vsum_ref, vdiff_ref, ci_ref, si_ref, o_ref,
    yre_ref, yim_ref,
):
    streams = x_ref.shape[0]
    group = streams // 2
    pad = c1_ref.shape[0]

    def dot(a, b):
        return jnp.dot(a, b, precision=PRECISION, preferred_element_type=jnp.float32)

    twc = twc_ref[...]
    tws = tws_ref[...]
    c1 = c1_ref[...]
    s1 = s1_ref[...]
    for j in range(streams):
        xj = x_ref[j]
        a = dot(c1, xj)
        b = dot(s1, xj)
        yre_ref[j * pad : (j + 1) * pad, :] = a * twc - b * tws
        yim_ref[j * pad : (j + 1) * pad, :] = a * tws + b * twc
    vc = vc_ref[...]
    vs = vs_ref[...]
    yre = yre_ref[...]
    yim = yim_ref[...]
    vsum = vsum_ref[...]
    ac = dot(yre, vc)
    bd = dot(yim, vs)
    zre = ac - bd
    zim = dot(yre + yim, vsum) - ac - bd
    half = group * pad
    pre = zre[:half] * zre[half:] - zim[:half] * zim[half:]
    pim = zre[:half] * zim[half:] + zim[:half] * zre[half:]
    vdiff = vdiff_ref[...]
    ac = dot(pre, vc)
    bd = dot(pim, vs)
    qre = ac + bd
    qim = dot(pre + pim, vdiff) - ac + bd
    ci = ci_ref[...]
    si = si_ref[...]
    for g in range(group):
        ure = qre[g * pad : (g + 1) * pad]
        uim = qim[g * pad : (g + 1) * pad]
        vre = ure * twc + uim * tws
        vim = uim * twc - ure * tws
        o_ref[g] = dot(ci, vre) - dot(si, vim)


def fused_kernel(shards, parts, src_ref, *refs):
    tables = refs[:10]
    out_ref, recv_ref, stage_ref = refs[10:13]
    x_ref, o_ref, yre_ref, yim_ref, sends, recvs, local = refs[13:]
    me = lax.axis_index("seq")
    row = lax.axis_index("ch")
    mesh_id = pl.DeviceIdType.MESH
    streams = x_ref.shape[0]
    barrier = pltpu.get_barrier_semaphore()

    def peer_of(step):
        return lax.rem(me + 1 + step, shards)

    def greet(step, carry):
        pl.semaphore_signal(barrier, inc=1, device_id=(peer_of(step), row), device_id_type=mesh_id)
        return carry

    lax.fori_loop(0, shards - 1, greet, 0)
    pl.semaphore_wait(barrier, shards - 1)

    def scatter(source, target, phase):
        own = pltpu.make_async_copy(source(me), target(me), local.at[phase])
        own.start()

        def copy_to(peer, slot):
            return pltpu.make_async_remote_copy(
                src_ref=source(peer),
                dst_ref=target(slot),
                send_sem=sends.at[phase, peer],
                recv_sem=recvs.at[phase, slot],
                device_id=(peer, row),
                device_id_type=mesh_id,
            )

        def send(step, carry):
            copy_to(peer_of(step), me).start()
            return carry

        lax.fori_loop(0, shards - 1, send, 0)

        def finish():
            def wait_one(step, carry):
                peer = peer_of(step)
                copy_to(peer, me).wait_send()
                copy_to(peer, peer).wait_recv()
                return carry

            lax.fori_loop(0, shards - 1, wait_one, 0)
            own.wait()

        return finish

    arrivals = [
        scatter(lambda j, h=h: src_ref.at[j, h], lambda j, h=h: recv_ref.at[j, h], h)
        for h in range(parts)
    ]
    returns = []
    for h in range(parts):
        arrivals[h]()
        gathers = [
            pltpu.make_async_copy(recv_ref.at[:, h, j, :], x_ref.at[j], local.at[2 * parts + j])
            for j in range(streams)
        ]
        for copy in gathers:
            copy.start()
        for copy in gathers:
            copy.wait()
        conv_body(x_ref, *tables, o_ref, yre_ref, yim_ref)
        put = pltpu.make_async_copy(o_ref, stage_ref.at[h], local.at[2 * parts + streams])
        put.start()
        put.wait()
        returns.append(
            scatter(
                lambda j, h=h: stage_ref.at[h, :, j, :],
                lambda j, h=h: out_ref.at[j, h],
                parts + h,
            )
        )
    for finish in returns:
        finish()


def long_conv(pieces):
    blocks, parts, streams, rows = pieces.shape
    group = streams // 2
    coarse = 2 * blocks
    total = coarse * rows
    half = blocks + 1
    pad = -(-half // 8) * 8
    live = (np.arange(pad) < half).astype(np.float64)
    c1, s1 = phase_table(pad, blocks, coarse, -1.0)
    c1 = c1 * live[:, None]
    s1 = s1 * live[:, None]
    twc, tws = phase_table(pad, rows, total, -1.0)
    vc, vs = phase_table(rows, rows, rows, -1.0)
    k1 = np.arange(pad)
    weight = np.where((k1 == 0) | (k1 == blocks), 1.0, 2.0) * live / total
    ci, si = phase_table(blocks, pad, coarse, 1.0)
    ci = ci * weight[None, :]
    si = si * weight[None, :]
    tables = [c1, s1, twc, tws, vc, vs, vc + vs, vc - vs, ci, si]
    tables = [jnp.asarray(t, dtype=jnp.float32) for t in tables]
    vmem = pl.BlockSpec(memory_space=pltpu.VMEM)
    anywhere = pl.BlockSpec(memory_space=pl.ANY)
    f32 = jnp.float32
    return pl.pallas_call(
        functools.partial(fused_kernel, blocks, parts),
        out_shape=[
            jax.ShapeDtypeStruct((blocks, parts, group, rows), f32),
            jax.ShapeDtypeStruct((blocks, parts, streams, rows), f32),
            jax.ShapeDtypeStruct((parts, group, blocks, rows), f32),
        ],
        in_specs=[anywhere] + [vmem] * len(tables),
        out_specs=[anywhere] * 3,
        scratch_shapes=[
            pltpu.VMEM((streams, blocks, rows), f32),
            pltpu.VMEM((group, blocks, rows), f32),
            pltpu.VMEM((streams * pad, rows), f32),
            pltpu.VMEM((streams * pad, rows), f32),
            pltpu.SemaphoreType.DMA((2 * parts, blocks)),
            pltpu.SemaphoreType.DMA((2 * parts, blocks)),
            pltpu.SemaphoreType.DMA((2 * parts + streams + 1,)),
        ],
        compiler_params=pltpu.CompilerParams(collective_id=0, has_side_effects=True),
    )(pieces, *tables)[0]


def shifted(block, axis, distance):
    devices = range(lax.axis_size(axis))
    route = [(i - distance, i) for i in devices if i - distance in devices]
    return lax.ppermute(block, axis, route)


def on_device(qkv, short_w, skip, filt):
    rows, _, width = qkv.shape
    taps = short_w.shape[0]
    shards = lax.axis_size("seq")
    group = width // shards
    rim = shifted(qkv[rows - (taps - 1) :], "seq", 1)
    extended = jnp.concatenate([rim, qkv], axis=0).astype(jnp.float32)
    feat = short_w[0] * extended[taps - 1 : taps - 1 + rows]
    for tap in range(1, taps):
        feat = feat + short_w[tap] * extended[taps - 1 - tap : taps - 1 - tap + rows]
    query = feat[:, 0, :]
    signal = feat[:, 1, :] * feat[:, 2, :]
    parts = 4
    source = jnp.stack([signal, filt]).reshape(2, rows, shards, parts, group // parts)
    source = source.transpose(2, 3, 0, 4, 1).reshape(shards, parts, 2 * group // parts, rows)
    values = long_conv(source)
    conv = values.reshape(width, rows).T
    return (query * (conv + skip * signal)).astype(jnp.bfloat16)


def solution(mesh):
    return jax.shard_map(
        on_device,
        mesh=mesh,
        in_specs=(P("seq", None, "ch"), P(None, None, "ch"), P("ch"), P("seq", "ch")),
        out_specs=P("seq", "ch"),
        check_vma=False,
    )
```

```python
import functools
import math

import jax
import numpy as np
import jax.numpy as jnp
from jax import lax
from jax.experimental import pallas as pl
from jax.experimental.pallas import tpu as pltpu
from jax.sharding import PartitionSpec as P

PRECISION = lax.Precision.HIGHEST


def phase_table(count_out, count_in, modulus, sign):
    phase = np.arange(count_out)[:, None] * np.arange(count_in)[None, :] % modulus
    angles = sign * 2.0 * np.pi / modulus * phase
    return np.cos(angles), np.sin(angles)


def conv_body(
    x_ref, c1_ref, s1_ref, twc_ref, tws_ref, vc_ref, vs_ref, vsum_ref, vdiff_ref, ci_ref, si_ref, o_ref,
    yre_ref, yim_ref,
):
    streams = x_ref.shape[0]
    group = streams // 2
    pad = c1_ref.shape[0]

    def dot(a, b):
        return jnp.dot(a, b, precision=PRECISION, preferred_element_type=jnp.float32)

    twc = twc_ref[...]
    tws = tws_ref[...]
    c1 = c1_ref[...]
    s1 = s1_ref[...]
    for j in range(streams):
        xj = x_ref[j]
        a = dot(c1, xj)
        b = dot(s1, xj)
        yre_ref[j * pad : (j + 1) * pad, :] = a * twc - b * tws
        yim_ref[j * pad : (j + 1) * pad, :] = a * tws + b * twc
    vc = vc_ref[...]
    vs = vs_ref[...]
    yre = yre_ref[...]
    yim = yim_ref[...]
    vsum = vsum_ref[...]
    ac = dot(yre, vc)
    bd = dot(yim, vs)
    zre = ac - bd
    zim = dot(yre + yim, vsum) - ac - bd
    half = group * pad
    pre = zre[:half] * zre[half:] - zim[:half] * zim[half:]
    pim = zre[:half] * zim[half:] + zim[:half] * zre[half:]
    vdiff = vdiff_ref[...]
    ac = dot(pre, vc)
    bd = dot(pim, vs)
    qre = ac + bd
    qim = dot(pre + pim, vdiff) - ac + bd
    ci = ci_ref[...]
    si = si_ref[...]
    for g in range(group):
        ure = qre[g * pad : (g + 1) * pad]
        uim = qim[g * pad : (g + 1) * pad]
        vre = ure * twc + uim * tws
        vim = uim * twc - ure * tws
        o_ref[g] = dot(ci, vre) - dot(si, vim)


def fused_kernel(shards, parts, src_ref, *refs):
    tables = refs[:10]
    out_ref, recv_ref, stage_ref = refs[10:13]
    x_ref, o_ref, yre_ref, yim_ref, sends, recvs, local = refs[13:]
    me = lax.axis_index("seq")
    row = lax.axis_index("ch")
    mesh_id = pl.DeviceIdType.MESH
    streams = x_ref.shape[0]
    barrier = pltpu.get_barrier_semaphore()

    def peer_of(step):
        distance = step // 2 + 1
        sign = 1 - 2 * (step % 2)
        return lax.rem(me + sign * distance + shards, shards)

    def greet(step, carry):
        pl.semaphore_signal(barrier, inc=1, device_id=(peer_of(step), row), device_id_type=mesh_id)
        return carry

    lax.fori_loop(0, shards - 1, greet, 0)
    pl.semaphore_wait(barrier, shards - 1)

    def scatter(source, target, phase):
        own = pltpu.make_async_copy(source(me), target(me), local.at[phase])
        own.start()

        def copy_to(peer, slot):
            return pltpu.make_async_remote_copy(
                src_ref=source(peer),
                dst_ref=target(slot),
                send_sem=sends.at[phase, peer],
                recv_sem=recvs.at[phase, slot],
                device_id=(peer, row),
                device_id_type=mesh_id,
            )

        def send(step, carry):
            copy_to(peer_of(step), me).start()
            return carry

        lax.fori_loop(0, shards - 1, send, 0)

        def finish():
            def wait_one(step, carry):
                peer = peer_of(step)
                copy_to(peer, me).wait_send()
                copy_to(peer, peer).wait_recv()
                return carry

            lax.fori_loop(0, shards - 1, wait_one, 0)
            own.wait()

        return finish

    arrivals = [
        scatter(lambda j, h=h: src_ref.at[j, h], lambda j, h=h: recv_ref.at[j, h], h)
        for h in range(parts)
    ]
    returns = []
    for h in range(parts):
        arrivals[h]()
        gathers = [
            pltpu.make_async_copy(recv_ref.at[:, h, j, :], x_ref.at[j], local.at[2 * parts + j])
            for j in range(streams)
        ]
        for copy in gathers:
            copy.start()
        for copy in gathers:
            copy.wait()
        conv_body(x_ref, *tables, o_ref, yre_ref, yim_ref)
        put = pltpu.make_async_copy(o_ref, stage_ref.at[h], local.at[2 * parts + streams])
        put.start()
        put.wait()
        returns.append(
            scatter(
                lambda j, h=h: stage_ref.at[h, :, j, :],
                lambda j, h=h: out_ref.at[j, h],
                parts + h,
            )
        )
    for finish in returns:
        finish()


def long_conv(pieces):
    blocks, parts, streams, rows = pieces.shape
    group = streams // 2
    coarse = 2 * blocks
    total = coarse * rows
    half = blocks + 1
    pad = -(-half // 8) * 8
    live = (np.arange(pad) < half).astype(np.float64)
    c1, s1 = phase_table(pad, blocks, coarse, -1.0)
    c1 = c1 * live[:, None]
    s1 = s1 * live[:, None]
    twc, tws = phase_table(pad, rows, total, -1.0)
    vc, vs = phase_table(rows, rows, rows, -1.0)
    k1 = np.arange(pad)
    weight = np.where((k1 == 0) | (k1 == blocks), 1.0, 2.0) * live / total
    ci, si = phase_table(blocks, pad, coarse, 1.0)
    ci = ci * weight[None, :]
    si = si * weight[None, :]
    tables = [c1, s1, twc, tws, vc, vs, vc + vs, vc - vs, ci, si]
    tables = [jnp.asarray(t, dtype=jnp.float32) for t in tables]
    vmem = pl.BlockSpec(memory_space=pltpu.VMEM)
    anywhere = pl.BlockSpec(memory_space=pl.ANY)
    f32 = jnp.float32
    return pl.pallas_call(
        functools.partial(fused_kernel, blocks, parts),
        out_shape=[
            jax.ShapeDtypeStruct((blocks, parts, group, rows), f32),
            jax.ShapeDtypeStruct((blocks, parts, streams, rows), f32),
            jax.ShapeDtypeStruct((parts, group, blocks, rows), f32),
        ],
        in_specs=[anywhere] + [vmem] * len(tables),
        out_specs=[anywhere] * 3,
        scratch_shapes=[
            pltpu.VMEM((streams, blocks, rows), f32),
            pltpu.VMEM((group, blocks, rows), f32),
            pltpu.VMEM((streams * pad, rows), f32),
            pltpu.VMEM((streams * pad, rows), f32),
            pltpu.SemaphoreType.DMA((2 * parts, blocks)),
            pltpu.SemaphoreType.DMA((2 * parts, blocks)),
            pltpu.SemaphoreType.DMA((2 * parts + streams + 1,)),
        ],
        compiler_params=pltpu.CompilerParams(collective_id=0, has_side_effects=True),
    )(pieces, *tables)[0]


def shifted(block, axis, distance):
    devices = range(lax.axis_size(axis))
    route = [(i - distance, i) for i in devices if i - distance in devices]
    return lax.ppermute(block, axis, route)


def on_device(qkv, short_w, skip, filt):
    rows, _, width = qkv.shape
    taps = short_w.shape[0]
    shards = lax.axis_size("seq")
    group = width // shards
    rim = shifted(qkv[rows - (taps - 1) :], "seq", 1)
    extended = jnp.concatenate([rim, qkv], axis=0).astype(jnp.float32)
    feat = short_w[0] * extended[taps - 1 : taps - 1 + rows]
    for tap in range(1, taps):
        feat = feat + short_w[tap] * extended[taps - 1 - tap : taps - 1 - tap + rows]
    query = feat[:, 0, :]
    signal = feat[:, 1, :] * feat[:, 2, :]
    parts = 2
    source = jnp.stack([signal, filt]).reshape(2, rows, shards, parts, group // parts)
    source = source.transpose(2, 3, 0, 4, 1).reshape(shards, parts, 2 * group // parts, rows)
    values = long_conv(source)
    conv = values.reshape(width, rows).T
    return (query * (conv + skip * signal)).astype(jnp.bfloat16)


def solution(mesh):
    return jax.shard_map(
        on_device,
        mesh=mesh,
        in_specs=(P("seq", None, "ch"), P(None, None, "ch"), P("ch"), P("seq", "ch")),
        out_specs=P("seq", "ch"),
        check_vma=False,
    )
```

```python
import functools
import math

import jax
import numpy as np
import jax.numpy as jnp
from jax import lax
from jax.experimental import pallas as pl
from jax.experimental.pallas import tpu as pltpu
from jax.sharding import PartitionSpec as P

PRECISION = lax.Precision.HIGHEST


def phase_table(count_out, count_in, modulus, sign):
    phase = np.arange(count_out)[:, None] * np.arange(count_in)[None, :] % modulus
    angles = sign * 2.0 * np.pi / modulus * phase
    return np.cos(angles), np.sin(angles)


def conv_body(
    x_ref, c1_ref, s1_ref, twc_ref, tws_ref, vc_ref, vs_ref, vsum_ref, vdiff_ref, ci_ref, si_ref, o_ref,
    yre_ref, yim_ref,
):
    streams = x_ref.shape[0]
    group = streams // 2
    pad = c1_ref.shape[0]

    def dot(a, b):
        return jnp.dot(a, b, precision=PRECISION, preferred_element_type=jnp.float32)

    twc = twc_ref[...]
    tws = tws_ref[...]
    c1 = c1_ref[...]
    s1 = s1_ref[...]
    for j in range(streams):
        xj = x_ref[j]
        a = dot(c1, xj)
        b = dot(s1, xj)
        yre_ref[j * pad : (j + 1) * pad, :] = a * twc - b * tws
        yim_ref[j * pad : (j + 1) * pad, :] = a * tws + b * twc
    vc = vc_ref[...]
    vs = vs_ref[...]
    yre = yre_ref[...]
    yim = yim_ref[...]
    vsum = vsum_ref[...]
    ac = dot(yre, vc)
    bd = dot(yim, vs)
    zre = ac - bd
    zim = dot(yre + yim, vsum) - ac - bd
    half = group * pad
    pre = zre[:half] * zre[half:] - zim[:half] * zim[half:]
    pim = zre[:half] * zim[half:] + zim[:half] * zre[half:]
    vdiff = vdiff_ref[...]
    ac = dot(pre, vc)
    bd = dot(pim, vs)
    qre = ac + bd
    qim = dot(pre + pim, vdiff) - ac + bd
    ci = ci_ref[...]
    si = si_ref[...]
    for g in range(group):
        ure = qre[g * pad : (g + 1) * pad]
        uim = qim[g * pad : (g + 1) * pad]
        vre = ure * twc + uim * tws
        vim = uim * twc - ure * tws
        o_ref[g] = dot(ci, vre) - dot(si, vim)


def fused_kernel(shards, sizes, *refs):
    parts = len(sizes)
    srcs = refs[:parts]
    tables = refs[parts : parts + 10]
    outs, recvs_hbm, stages = (refs[parts + 10 + k * parts : parts + 10 + (k + 1) * parts] for k in range(3))
    x_all, o_all, yre_all, yim_all, sends, recvs, local = refs[parts + 10 + 3 * parts :]
    me = lax.axis_index("seq")
    row = lax.axis_index("ch")
    mesh_id = pl.DeviceIdType.MESH
    barrier = pltpu.get_barrier_semaphore()

    def peer_of(step):
        distance = step // 2 + 1
        sign = 1 - 2 * (step % 2)
        return lax.rem(me + sign * distance + shards, shards)

    def greet(step, carry):
        pl.semaphore_signal(barrier, inc=1, device_id=(peer_of(step), row), device_id_type=mesh_id)
        return carry

    lax.fori_loop(0, shards - 1, greet, 0)
    pl.semaphore_wait(barrier, shards - 1)

    def scatter(source, target, phase):
        own = pltpu.make_async_copy(source(me), target(me), local.at[phase])
        own.start()

        def copy_to(peer, slot):
            return pltpu.make_async_remote_copy(
                src_ref=source(peer),
                dst_ref=target(slot),
                send_sem=sends.at[phase, peer],
                recv_sem=recvs.at[phase, slot],
                device_id=(peer, row),
                device_id_type=mesh_id,
            )

        def send(step, carry):
            copy_to(peer_of(step), me).start()
            return carry

        lax.fori_loop(0, shards - 1, send, 0)

        def finish():
            def wait_one(step, carry):
                peer = peer_of(step)
                copy_to(peer, me).wait_send()
                copy_to(peer, peer).wait_recv()
                return carry

            lax.fori_loop(0, shards - 1, wait_one, 0)
            own.wait()

        return finish

    arrivals = [
        scatter(lambda j, h=h: srcs[h].at[j], lambda j, h=h: recvs_hbm[h].at[j], h)
        for h in range(parts)
    ]
    returns = []
    pad = tables[0].shape[0]
    for h in range(parts):
        streams = 2 * sizes[h]
        x_ref = x_all.at[pl.ds(0, streams)]
        o_ref = o_all.at[pl.ds(0, sizes[h])]
        yre_ref = yre_all.at[pl.ds(0, streams * pad)]
        yim_ref = yim_all.at[pl.ds(0, streams * pad)]
        arrivals[h]()
        gathers = [
            pltpu.make_async_copy(recvs_hbm[h].at[:, j, :], x_ref.at[j], local.at[2 * parts + j])
            for j in range(streams)
        ]
        for copy in gathers:
            copy.start()
        for copy in gathers:
            copy.wait()
        conv_body(x_ref, *tables, o_ref, yre_ref, yim_ref)
        put = pltpu.make_async_copy(o_ref, stages[h], local.at[2 * parts + 2 * max(sizes)])
        put.start()
        put.wait()
        returns.append(
            scatter(
                lambda j, h=h: stages[h].at[:, j, :],
                lambda j, h=h: outs[h].at[j],
                parts + h,
            )
        )
    for finish in returns:
        finish()


def long_conv(pieces):
    blocks, _, rows = pieces[0].shape
    sizes = tuple(p.shape[1] // 2 for p in pieces)
    group = max(sizes)
    streams = 2 * group
    parts = len(sizes)
    coarse = 2 * blocks
    total = coarse * rows
    half = blocks + 1
    pad = -(-half // 8) * 8
    live = (np.arange(pad) < half).astype(np.float64)
    c1, s1 = phase_table(pad, blocks, coarse, -1.0)
    c1 = c1 * live[:, None]
    s1 = s1 * live[:, None]
    twc, tws = phase_table(pad, rows, total, -1.0)
    vc, vs = phase_table(rows, rows, rows, -1.0)
    k1 = np.arange(pad)
    weight = np.where((k1 == 0) | (k1 == blocks), 1.0, 2.0) * live / total
    ci, si = phase_table(blocks, pad, coarse, 1.0)
    ci = ci * weight[None, :]
    si = si * weight[None, :]
    tables = [c1, s1, twc, tws, vc, vs, vc + vs, vc - vs, ci, si]
    tables = [jnp.asarray(t, dtype=jnp.float32) for t in tables]
    vmem = pl.BlockSpec(memory_space=pltpu.VMEM)
    anywhere = pl.BlockSpec(memory_space=pl.ANY)
    f32 = jnp.float32
    return pl.pallas_call(
        functools.partial(fused_kernel, blocks, sizes),
        out_shape=[jax.ShapeDtypeStruct((blocks, s, rows), f32) for s in sizes]
        + [jax.ShapeDtypeStruct((blocks, 2 * s, rows), f32) for s in sizes]
        + [jax.ShapeDtypeStruct((s, blocks, rows), f32) for s in sizes],
        in_specs=[anywhere] * parts + [vmem] * len(tables),
        out_specs=[anywhere] * (3 * parts),
        scratch_shapes=[
            pltpu.VMEM((streams, blocks, rows), f32),
            pltpu.VMEM((group, blocks, rows), f32),
            pltpu.VMEM((streams * pad, rows), f32),
            pltpu.VMEM((streams * pad, rows), f32),
            pltpu.SemaphoreType.DMA((2 * parts, blocks)),
            pltpu.SemaphoreType.DMA((2 * parts, blocks)),
            pltpu.SemaphoreType.DMA((2 * parts + streams + 1,)),
        ],
        compiler_params=pltpu.CompilerParams(collective_id=0, has_side_effects=True),
    )(*pieces, *tables)[:parts]


def shifted(block, axis, distance):
    devices = range(lax.axis_size(axis))
    route = [(i - distance, i) for i in devices if i - distance in devices]
    return lax.ppermute(block, axis, route)


def on_device(qkv, short_w, skip, filt):
    rows, _, width = qkv.shape
    taps = short_w.shape[0]
    shards = lax.axis_size("seq")
    group = width // shards
    rim = shifted(qkv[rows - (taps - 1) :], "seq", 1)
    extended = jnp.concatenate([rim, qkv], axis=0).astype(jnp.float32)
    feat = short_w[0] * extended[taps - 1 : taps - 1 + rows]
    for tap in range(1, taps):
        feat = feat + short_w[tap] * extended[taps - 1 - tap : taps - 1 - tap + rows]
    query = feat[:, 0, :]
    signal = feat[:, 1, :] * feat[:, 2, :]
    sizes = (group - group * 3 // 8, group * 3 // 8)
    source = jnp.stack([signal, filt]).reshape(2, rows, shards, group)
    pieces, start = [], 0
    for size in sizes:
        piece = source[:, :, :, start : start + size].transpose(2, 0, 3, 1)
        pieces.append(piece.reshape(shards, 2 * size, rows))
        start += size
    values = jnp.concatenate(long_conv(pieces), axis=1)
    conv = values.reshape(width, rows).T
    return (query * (conv + skip * signal)).astype(jnp.bfloat16)


def solution(mesh):
    return jax.shard_map(
        on_device,
        mesh=mesh,
        in_specs=(P("seq", None, "ch"), P(None, None, "ch"), P("ch"), P("seq", "ch")),
        out_specs=P("seq", "ch"),
        check_vma=False,
    )
```

```python
import functools
import math

import jax
import numpy as np
import jax.numpy as jnp
from jax import lax
from jax.experimental import pallas as pl
from jax.experimental.pallas import tpu as pltpu
from jax.sharding import PartitionSpec as P

PRECISION = lax.Precision.HIGHEST


def phase_table(count_out, count_in, modulus, sign):
    phase = np.arange(count_out)[:, None] * np.arange(count_in)[None, :] % modulus
    angles = sign * 2.0 * np.pi / modulus * phase
    return np.cos(angles), np.sin(angles)


def conv_body(
    x_ref, c1_ref, s1_ref, twc_ref, tws_ref, vc_ref, vs_ref, vsum_ref, vdiff_ref, ci_ref, si_ref, o_ref,
    yre_ref, yim_ref,
):
    streams = x_ref.shape[0]
    group = streams // 2
    pad = c1_ref.shape[0]

    def dot(a, b):
        return jnp.dot(a, b, precision=PRECISION, preferred_element_type=jnp.float32)

    twc = twc_ref[...]
    tws = tws_ref[...]
    c1 = c1_ref[...]
    s1 = s1_ref[...]
    for j in range(streams):
        xj = x_ref[j]
        a = dot(c1, xj)
        b = dot(s1, xj)
        yre_ref[j * pad : (j + 1) * pad, :] = a * twc - b * tws
        yim_ref[j * pad : (j + 1) * pad, :] = a * tws + b * twc
    vc = vc_ref[...]
    vs = vs_ref[...]
    yre = yre_ref[...]
    yim = yim_ref[...]
    vsum = vsum_ref[...]
    ac = dot(yre, vc)
    bd = dot(yim, vs)
    zre = ac - bd
    zim = dot(yre + yim, vsum) - ac - bd
    half = group * pad
    pre = zre[:half] * zre[half:] - zim[:half] * zim[half:]
    pim = zre[:half] * zim[half:] + zim[:half] * zre[half:]
    vdiff = vdiff_ref[...]
    ac = dot(pre, vc)
    bd = dot(pim, vs)
    qre = ac + bd
    qim = dot(pre + pim, vdiff) - ac + bd
    ci = ci_ref[...]
    si = si_ref[...]
    for g in range(group):
        ure = qre[g * pad : (g + 1) * pad]
        uim = qim[g * pad : (g + 1) * pad]
        vre = ure * twc + uim * tws
        vim = uim * twc - ure * tws
        o_ref[g] = dot(ci, vre) - dot(si, vim)


def fused_kernel(shards, parts, src_ref, *refs):
    tables = refs[:10]
    out_ref, recv_ref, stage_ref = refs[10:13]
    x_ref, o_ref, yre_ref, yim_ref, sends, recvs, local = refs[13:]
    me = lax.axis_index("seq")
    row = lax.axis_index("ch")
    mesh_id = pl.DeviceIdType.MESH
    streams = x_ref.shape[0]
    size = streams // 2
    barrier = pltpu.get_barrier_semaphore()

    def peer_of(step):
        distance = step // 2 + 1
        sign = 1 - 2 * (step % 2)
        return lax.rem(me + sign * distance + shards, shards)

    def greet(step, carry):
        pl.semaphore_signal(barrier, inc=1, device_id=(peer_of(step), row), device_id_type=mesh_id)
        return carry

    lax.fori_loop(0, shards - 1, greet, 0)
    pl.semaphore_wait(barrier, shards - 1)

    def scatter(source, target, phase):
        own = pltpu.make_async_copy(source(me), target(me), local.at[phase])
        own.start()

        def copy_to(peer, slot):
            return pltpu.make_async_remote_copy(
                src_ref=source(peer),
                dst_ref=target(slot),
                send_sem=sends.at[phase, peer],
                recv_sem=recvs.at[phase, slot],
                device_id=(peer, row),
                device_id_type=mesh_id,
            )

        def send(step, carry):
            copy_to(peer_of(step), me).start()
            return carry

        lax.fori_loop(0, shards - 1, send, 0)

        def finish():
            def wait_one(step, carry):
                peer = peer_of(step)
                copy_to(peer, me).wait_send()
                copy_to(peer, peer).wait_recv()
                return carry

            lax.fori_loop(0, shards - 1, wait_one, 0)
            own.wait()

        return finish

    arrivals = [
        scatter(
            lambda j, h=h: src_ref.at[j, :, pl.ds(h * size, size), :],
            lambda j, h=h: recv_ref.at[j, h],
            h,
        )
        for h in range(parts)
    ]
    returns = []
    for h in range(parts):
        arrivals[h]()
        gathers = [
            pltpu.make_async_copy(
                recv_ref.at[:, h, j // size, j % size, :], x_ref.at[j], local.at[2 * parts + j]
            )
            for j in range(streams)
        ]
        for copy in gathers:
            copy.start()
        for copy in gathers:
            copy.wait()
        conv_body(x_ref, *tables, o_ref, yre_ref, yim_ref)
        put = pltpu.make_async_copy(o_ref, stage_ref.at[h], local.at[2 * parts + streams])
        put.start()
        put.wait()
        returns.append(
            scatter(
                lambda j, h=h: stage_ref.at[h, :, j, :],
                lambda j, h=h: out_ref.at[j, pl.ds(h * size, size), :],
                parts + h,
            )
        )
    for finish in returns:
        finish()


def long_conv(pieces, parts):
    blocks, _, channels, rows = pieces.shape
    group = channels // parts
    streams = 2 * group
    coarse = 2 * blocks
    total = coarse * rows
    half = blocks + 1
    pad = -(-half // 8) * 8
    live = (np.arange(pad) < half).astype(np.float64)
    c1, s1 = phase_table(pad, blocks, coarse, -1.0)
    c1 = c1 * live[:, None]
    s1 = s1 * live[:, None]
    twc, tws = phase_table(pad, rows, total, -1.0)
    vc, vs = phase_table(rows, rows, rows, -1.0)
    k1 = np.arange(pad)
    weight = np.where((k1 == 0) | (k1 == blocks), 1.0, 2.0) * live / total
    ci, si = phase_table(blocks, pad, coarse, 1.0)
    ci = ci * weight[None, :]
    si = si * weight[None, :]
    tables = [c1, s1, twc, tws, vc, vs, vc + vs, vc - vs, ci, si]
    tables = [jnp.asarray(t, dtype=jnp.float32) for t in tables]
    vmem = pl.BlockSpec(memory_space=pltpu.VMEM)
    anywhere = pl.BlockSpec(memory_space=pl.ANY)
    f32 = jnp.float32
    return pl.pallas_call(
        functools.partial(fused_kernel, blocks, parts),
        out_shape=[
            jax.ShapeDtypeStruct((blocks, channels, rows), f32),
            jax.ShapeDtypeStruct((blocks, parts, 2, group, rows), f32),
            jax.ShapeDtypeStruct((parts, group, blocks, rows), f32),
        ],
        in_specs=[anywhere] + [vmem] * len(tables),
        out_specs=[anywhere] * 3,
        scratch_shapes=[
            pltpu.VMEM((streams, blocks, rows), f32),
            pltpu.VMEM((group, blocks, rows), f32),
            pltpu.VMEM((streams * pad, rows), f32),
            pltpu.VMEM((streams * pad, rows), f32),
            pltpu.SemaphoreType.DMA((2 * parts, blocks)),
            pltpu.SemaphoreType.DMA((2 * parts, blocks)),
            pltpu.SemaphoreType.DMA((2 * parts + streams + 1,)),
        ],
        compiler_params=pltpu.CompilerParams(collective_id=0, has_side_effects=True),
    )(pieces, *tables)[0]


def shifted(block, axis, distance):
    devices = range(lax.axis_size(axis))
    route = [(i - distance, i) for i in devices if i - distance in devices]
    return lax.ppermute(block, axis, route)


def on_device(qkv, short_w, skip, filt):
    rows, _, width = qkv.shape
    taps = short_w.shape[0]
    shards = lax.axis_size("seq")
    group = width // shards
    rim = shifted(qkv[rows - (taps - 1) :], "seq", 1)
    extended = jnp.concatenate([rim, qkv], axis=0).astype(jnp.float32)
    feat = short_w[0] * extended[taps - 1 : taps - 1 + rows]
    for tap in range(1, taps):
        feat = feat + short_w[tap] * extended[taps - 1 - tap : taps - 1 - tap + rows]
    query = feat[:, 0, :]
    signal = feat[:, 1, :] * feat[:, 2, :]
    source = jnp.stack([signal, filt]).reshape(2, rows, shards, group).transpose(2, 0, 3, 1)
    values = long_conv(source, 2)
    conv = values.reshape(width, rows).T
    return (query * (conv + skip * signal)).astype(jnp.bfloat16)


def solution(mesh):
    return jax.shard_map(
        on_device,
        mesh=mesh,
        in_specs=(P("seq", None, "ch"), P(None, None, "ch"), P("ch"), P("seq", "ch")),
        out_specs=P("seq", "ch"),
        check_vma=False,
    )
```

```python
import functools
import math

import jax
import numpy as np
import jax.numpy as jnp
from jax import lax
from jax.experimental import pallas as pl
from jax.experimental.pallas import tpu as pltpu
from jax.sharding import PartitionSpec as P

PRECISION = lax.Precision.HIGHEST


def phase_table(count_out, count_in, modulus, sign):
    phase = np.arange(count_out)[:, None] * np.arange(count_in)[None, :] % modulus
    angles = sign * 2.0 * np.pi / modulus * phase
    return np.cos(angles), np.sin(angles)


def conv_body(
    x_ref, c1_ref, s1_ref, twc_ref, tws_ref, vc_ref, vs_ref, vsum_ref, vdiff_ref, ci_ref, si_ref, o_ref,
    yre_ref, yim_ref,
):
    streams = x_ref.shape[0]
    group = streams // 2
    pad = c1_ref.shape[0]

    def dot(a, b):
        return jnp.dot(a, b, precision=PRECISION, preferred_element_type=jnp.float32)

    twc = twc_ref[...]
    tws = tws_ref[...]
    c1 = c1_ref[...]
    s1 = s1_ref[...]
    for j in range(streams):
        xj = x_ref[j]
        a = dot(c1, xj)
        b = dot(s1, xj)
        yre_ref[j * pad : (j + 1) * pad, :] = a * twc - b * tws
        yim_ref[j * pad : (j + 1) * pad, :] = a * tws + b * twc
    vc = vc_ref[...]
    vs = vs_ref[...]
    yre = yre_ref[...]
    yim = yim_ref[...]
    vsum = vsum_ref[...]
    ac = dot(yre, vc)
    bd = dot(yim, vs)
    zre = ac - bd
    zim = dot(yre + yim, vsum) - ac - bd
    half = group * pad
    pre = zre[:half] * zre[half:] - zim[:half] * zim[half:]
    pim = zre[:half] * zim[half:] + zim[:half] * zre[half:]
    vdiff = vdiff_ref[...]
    ac = dot(pre, vc)
    bd = dot(pim, vs)
    qre = ac + bd
    qim = dot(pre + pim, vdiff) - ac + bd
    ci = ci_ref[...]
    si = si_ref[...]
    for g in range(group):
        ure = qre[g * pad : (g + 1) * pad]
        uim = qim[g * pad : (g + 1) * pad]
        vre = ure * twc + uim * tws
        vim = uim * twc - ure * tws
        o_ref[g] = dot(ci, vre) - dot(si, vim)


def fused_kernel(shards, parts, sig_ref, filt_ref, *refs):
    tables = refs[:10]
    res_ref, out_ref, recv_ref, stage_ref, src_ref = refs[10:15]
    srcv_ref, outv_ref, x_ref, o_ref, yre_ref, yim_ref, sends, recvs, local = refs[15:]
    me = lax.axis_index("seq")
    row = lax.axis_index("ch")
    mesh_id = pl.DeviceIdType.MESH
    streams = x_ref.shape[0]
    size = streams // 2
    barrier = pltpu.get_barrier_semaphore()

    def peer_of(step):
        distance = step // 2 + 1
        sign = 1 - 2 * (step % 2)
        return lax.rem(me + sign * distance + shards, shards)

    def greet(step, carry):
        pl.semaphore_signal(barrier, inc=1, device_id=(peer_of(step), row), device_id_type=mesh_id)
        return carry

    lax.fori_loop(0, shards - 1, greet, 0)
    chunk = srcv_ref.shape[1:]
    srcv_ref[:, 0] = sig_ref[...].T.reshape(shards, *chunk[1:])
    srcv_ref[:, 1] = filt_ref[...].T.reshape(shards, *chunk[1:])
    fill = pltpu.make_async_copy(srcv_ref, src_ref, local.at[2 * parts + streams + 1])
    fill.start()
    fill.wait()
    pl.semaphore_wait(barrier, shards - 1)

    def scatter(source, target, phase):
        own = pltpu.make_async_copy(source(me), target(me), local.at[phase])
        own.start()

        def copy_to(peer, slot):
            return pltpu.make_async_remote_copy(
                src_ref=source(peer),
                dst_ref=target(slot),
                send_sem=sends.at[phase, peer],
                recv_sem=recvs.at[phase, slot],
                device_id=(peer, row),
                device_id_type=mesh_id,
            )

        def send(step, carry):
            copy_to(peer_of(step), me).start()
            return carry

        lax.fori_loop(0, shards - 1, send, 0)

        def finish():
            def wait_one(step, carry):
                peer = peer_of(step)
                copy_to(peer, me).wait_send()
                copy_to(peer, peer).wait_recv()
                return carry

            lax.fori_loop(0, shards - 1, wait_one, 0)
            own.wait()

        return finish

    arrivals = [
        scatter(
            lambda j, h=h: src_ref.at[j, :, pl.ds(h * size, size), :],
            lambda j, h=h: recv_ref.at[j, h],
            h,
        )
        for h in range(parts)
    ]
    returns = []
    for h in range(parts):
        arrivals[h]()
        gathers = [
            pltpu.make_async_copy(
                recv_ref.at[:, h, j // size, j % size, :], x_ref.at[j], local.at[2 * parts + j]
            )
            for j in range(streams)
        ]
        for copy in gathers:
            copy.start()
        for copy in gathers:
            copy.wait()
        conv_body(x_ref, *tables, o_ref, yre_ref, yim_ref)
        put = pltpu.make_async_copy(o_ref, stage_ref.at[h], local.at[2 * parts + streams])
        put.start()
        put.wait()
        returns.append(
            scatter(
                lambda j, h=h: stage_ref.at[h, :, j, :],
                lambda j, h=h: out_ref.at[j, pl.ds(h * size, size), :],
                parts + h,
            )
        )
    for finish in returns:
        finish()
    drain = pltpu.make_async_copy(out_ref, outv_ref, local.at[2 * parts + streams + 2])
    drain.start()
    drain.wait()
    res_ref[...] = outv_ref[...].reshape(res_ref.shape[1], res_ref.shape[0]).T


def long_conv(signal, filt, blocks, parts):
    rows, width = signal.shape
    channels = width // blocks
    group = channels // parts
    streams = 2 * group
    coarse = 2 * blocks
    total = coarse * rows
    half = blocks + 1
    pad = -(-half // 8) * 8
    live = (np.arange(pad) < half).astype(np.float64)
    c1, s1 = phase_table(pad, blocks, coarse, -1.0)
    c1 = c1 * live[:, None]
    s1 = s1 * live[:, None]
    twc, tws = phase_table(pad, rows, total, -1.0)
    vc, vs = phase_table(rows, rows, rows, -1.0)
    k1 = np.arange(pad)
    weight = np.where((k1 == 0) | (k1 == blocks), 1.0, 2.0) * live / total
    ci, si = phase_table(blocks, pad, coarse, 1.0)
    ci = ci * weight[None, :]
    si = si * weight[None, :]
    tables = [c1, s1, twc, tws, vc, vs, vc + vs, vc - vs, ci, si]
    tables = [jnp.asarray(t, dtype=jnp.float32) for t in tables]
    vmem = pl.BlockSpec(memory_space=pltpu.VMEM)
    anywhere = pl.BlockSpec(memory_space=pl.ANY)
    f32 = jnp.float32
    return pl.pallas_call(
        functools.partial(fused_kernel, blocks, parts),
        out_shape=[
            jax.ShapeDtypeStruct((rows, width), f32),
            jax.ShapeDtypeStruct((blocks, channels, rows), f32),
            jax.ShapeDtypeStruct((blocks, parts, 2, group, rows), f32),
            jax.ShapeDtypeStruct((parts, group, blocks, rows), f32),
            jax.ShapeDtypeStruct((blocks, 2, channels, rows), f32),
        ],
        in_specs=[vmem] * (2 + len(tables)),
        out_specs=[vmem] + [anywhere] * 4,
        scratch_shapes=[
            pltpu.VMEM((blocks, 2, channels, rows), f32),
            pltpu.VMEM((blocks, channels, rows), f32),
            pltpu.VMEM((streams, blocks, rows), f32),
            pltpu.VMEM((group, blocks, rows), f32),
            pltpu.VMEM((streams * pad, rows), f32),
            pltpu.VMEM((streams * pad, rows), f32),
            pltpu.SemaphoreType.DMA((2 * parts, blocks)),
            pltpu.SemaphoreType.DMA((2 * parts, blocks)),
            pltpu.SemaphoreType.DMA((2 * parts + streams + 3,)),
        ],
        compiler_params=pltpu.CompilerParams(collective_id=0, has_side_effects=True),
    )(signal, filt, *tables)[0]


def shifted(block, axis, distance):
    devices = range(lax.axis_size(axis))
    route = [(i - distance, i) for i in devices if i - distance in devices]
    return lax.ppermute(block, axis, route)


def on_device(qkv, short_w, skip, filt):
    rows, _, width = qkv.shape
    taps = short_w.shape[0]
    shards = lax.axis_size("seq")
    group = width // shards
    rim = shifted(qkv[rows - (taps - 1) :], "seq", 1)
    extended = jnp.concatenate([rim, qkv], axis=0).astype(jnp.float32)
    feat = short_w[0] * extended[taps - 1 : taps - 1 + rows]
    for tap in range(1, taps):
        feat = feat + short_w[tap] * extended[taps - 1 - tap : taps - 1 - tap + rows]
    query = feat[:, 0, :]
    signal = feat[:, 1, :] * feat[:, 2, :]
    conv = long_conv(signal, filt, shards, 2)
    return (query * (conv + skip * signal)).astype(jnp.bfloat16)


def solution(mesh):
    return jax.shard_map(
        on_device,
        mesh=mesh,
        in_specs=(P("seq", None, "ch"), P(None, None, "ch"), P("ch"), P("seq", "ch")),
        out_specs=P("seq", "ch"),
        check_vma=False,
    )
```

```python
import functools
import math

import jax
import numpy as np
import jax.numpy as jnp
from jax import lax
from jax.experimental import pallas as pl
from jax.experimental.pallas import tpu as pltpu
from jax.sharding import PartitionSpec as P

PRECISION = lax.Precision.HIGH


def phase_table(count_out, count_in, modulus, sign):
    phase = np.arange(count_out)[:, None] * np.arange(count_in)[None, :] % modulus
    angles = sign * 2.0 * np.pi / modulus * phase
    return np.cos(angles), np.sin(angles)


def conv_body(
    x_ref, c1_ref, s1_ref, twc_ref, tws_ref, vc_ref, vs_ref, vsum_ref, vdiff_ref, ci_ref, si_ref, o_ref,
    yre_ref, yim_ref,
):
    streams = x_ref.shape[0]
    group = streams // 2
    pad = c1_ref.shape[0]

    def dot(a, b):
        return jnp.dot(a, b, precision=PRECISION, preferred_element_type=jnp.float32)

    twc = twc_ref[...]
    tws = tws_ref[...]
    c1 = c1_ref[...]
    s1 = s1_ref[...]
    for j in range(streams):
        xj = x_ref[j]
        a = dot(c1, xj)
        b = dot(s1, xj)
        yre_ref[j * pad : (j + 1) * pad, :] = a * twc - b * tws
        yim_ref[j * pad : (j + 1) * pad, :] = a * tws + b * twc
    vc = vc_ref[...]
    vs = vs_ref[...]
    yre = yre_ref[...]
    yim = yim_ref[...]
    vsum = vsum_ref[...]
    ac = dot(yre, vc)
    bd = dot(yim, vs)
    zre = ac - bd
    zim = dot(yre + yim, vsum) - ac - bd
    half = group * pad
    pre = zre[:half] * zre[half:] - zim[:half] * zim[half:]
    pim = zre[:half] * zim[half:] + zim[:half] * zre[half:]
    vdiff = vdiff_ref[...]
    ac = dot(pre, vc)
    bd = dot(pim, vs)
    qre = ac + bd
    qim = dot(pre + pim, vdiff) - ac + bd
    ci = ci_ref[...]
    si = si_ref[...]
    for g in range(group):
        ure = qre[g * pad : (g + 1) * pad]
        uim = qim[g * pad : (g + 1) * pad]
        vre = ure * twc + uim * tws
        vim = uim * twc - ure * tws
        o_ref[g] = dot(ci, vre) - dot(si, vim)


def fused_kernel(shards, parts, src_ref, *refs):
    tables = refs[:10]
    out_ref, recv_ref, stage_ref = refs[10:13]
    x_ref, o_ref, yre_ref, yim_ref, sends, recvs, local = refs[13:]
    me = lax.axis_index("seq")
    row = lax.axis_index("ch")
    mesh_id = pl.DeviceIdType.MESH
    streams = x_ref.shape[0]
    size = streams // 2
    barrier = pltpu.get_barrier_semaphore()

    def peer_of(step):
        distance = step // 2 + 1
        sign = 1 - 2 * (step % 2)
        return lax.rem(me + sign * distance + shards, shards)

    def greet(step, carry):
        pl.semaphore_signal(barrier, inc=1, device_id=(peer_of(step), row), device_id_type=mesh_id)
        return carry

    lax.fori_loop(0, shards - 1, greet, 0)
    pl.semaphore_wait(barrier, shards - 1)

    def scatter(source, target, phase):
        own = pltpu.make_async_copy(source(me), target(me), local.at[phase])
        own.start()

        def copy_to(peer, slot):
            return pltpu.make_async_remote_copy(
                src_ref=source(peer),
                dst_ref=target(slot),
                send_sem=sends.at[phase, peer],
                recv_sem=recvs.at[phase, slot],
                device_id=(peer, row),
                device_id_type=mesh_id,
            )

        def send(step, carry):
            copy_to(peer_of(step), me).start()
            return carry

        lax.fori_loop(0, shards - 1, send, 0)

        def finish():
            def wait_one(step, carry):
                peer = peer_of(step)
                copy_to(peer, me).wait_send()
                copy_to(peer, peer).wait_recv()
                return carry

            lax.fori_loop(0, shards - 1, wait_one, 0)
            own.wait()

        return finish

    arrivals = [
        scatter(
            lambda j, h=h: src_ref.at[j, :, pl.ds(h * size, size), :],
            lambda j, h=h: recv_ref.at[j, h],
            h,
        )
        for h in range(parts)
    ]
    returns = []
    for h in range(parts):
        arrivals[h]()
        gathers = [
            pltpu.make_async_copy(
                recv_ref.at[:, h, j // size, j % size, :], x_ref.at[j], local.at[2 * parts + j]
            )
            for j in range(streams)
        ]
        for copy in gathers:
            copy.start()
        for copy in gathers:
            copy.wait()
        conv_body(x_ref, *tables, o_ref, yre_ref, yim_ref)
        put = pltpu.make_async_copy(o_ref, stage_ref.at[h], local.at[2 * parts + streams])
        put.start()
        put.wait()
        returns.append(
            scatter(
                lambda j, h=h: stage_ref.at[h, :, j, :],
                lambda j, h=h: out_ref.at[j, pl.ds(h * size, size), :],
                parts + h,
            )
        )
    for finish in returns:
        finish()


def long_conv(pieces, parts):
    blocks, _, channels, rows = pieces.shape
    group = channels // parts
    streams = 2 * group
    coarse = 2 * blocks
    total = coarse * rows
    half = blocks + 1
    pad = -(-half // 8) * 8
    live = (np.arange(pad) < half).astype(np.float64)
    c1, s1 = phase_table(pad, blocks, coarse, -1.0)
    c1 = c1 * live[:, None]
    s1 = s1 * live[:, None]
    twc, tws = phase_table(pad, rows, total, -1.0)
    vc, vs = phase_table(rows, rows, rows, -1.0)
    k1 = np.arange(pad)
    weight = np.where((k1 == 0) | (k1 == blocks), 1.0, 2.0) * live / total
    ci, si = phase_table(blocks, pad, coarse, 1.0)
    ci = ci * weight[None, :]
    si = si * weight[None, :]
    tables = [c1, s1, twc, tws, vc, vs, vc + vs, vc - vs, ci, si]
    tables = [jnp.asarray(t, dtype=jnp.float32) for t in tables]
    vmem = pl.BlockSpec(memory_space=pltpu.VMEM)
    anywhere = pl.BlockSpec(memory_space=pl.ANY)
    f32 = jnp.float32
    return pl.pallas_call(
        functools.partial(fused_kernel, blocks, parts),
        out_shape=[
            jax.ShapeDtypeStruct((blocks, channels, rows), f32),
            jax.ShapeDtypeStruct((blocks, parts, 2, group, rows), f32),
            jax.ShapeDtypeStruct((parts, group, blocks, rows), f32),
        ],
        in_specs=[anywhere] + [vmem] * len(tables),
        out_specs=[anywhere] * 3,
        scratch_shapes=[
            pltpu.VMEM((streams, blocks, rows), f32),
            pltpu.VMEM((group, blocks, rows), f32),
            pltpu.VMEM((streams * pad, rows), f32),
            pltpu.VMEM((streams * pad, rows), f32),
            pltpu.SemaphoreType.DMA((2 * parts, blocks)),
            pltpu.SemaphoreType.DMA((2 * parts, blocks)),
            pltpu.SemaphoreType.DMA((2 * parts + streams + 1,)),
        ],
        compiler_params=pltpu.CompilerParams(collective_id=0, has_side_effects=True),
    )(pieces, *tables)[0]


def shifted(block, axis, distance):
    devices = range(lax.axis_size(axis))
    route = [(i - distance, i) for i in devices if i - distance in devices]
    return lax.ppermute(block, axis, route)


def on_device(qkv, short_w, skip, filt):
    rows, _, width = qkv.shape
    taps = short_w.shape[0]
    shards = lax.axis_size("seq")
    group = width // shards
    rim = shifted(qkv[rows - (taps - 1) :], "seq", 1)
    extended = jnp.concatenate([rim, qkv], axis=0).astype(jnp.float32)
    feat = short_w[0] * extended[taps - 1 : taps - 1 + rows]
    for tap in range(1, taps):
        feat = feat + short_w[tap] * extended[taps - 1 - tap : taps - 1 - tap + rows]
    query = feat[:, 0, :]
    signal = feat[:, 1, :] * feat[:, 2, :]
    source = jnp.stack([signal, filt]).reshape(2, rows, shards, group).transpose(2, 0, 3, 1)
    values = long_conv(source, 2)
    conv = values.reshape(width, rows).T
    return (query * (conv + skip * signal)).astype(jnp.bfloat16)


def solution(mesh):
    return jax.shard_map(
        on_device,
        mesh=mesh,
        in_specs=(P("seq", None, "ch"), P(None, None, "ch"), P("ch"), P("seq", "ch")),
        out_specs=P("seq", "ch"),
        check_vma=False,
    )
```

```python
import functools
import math

import jax
import numpy as np
import jax.numpy as jnp
from jax import lax
from jax.experimental import pallas as pl
from jax.experimental.pallas import tpu as pltpu
from jax.sharding import PartitionSpec as P

PRECISION = lax.Precision.HIGHEST


def phase_table(count_out, count_in, modulus, sign):
    phase = np.arange(count_out)[:, None] * np.arange(count_in)[None, :] % modulus
    angles = sign * 2.0 * np.pi / modulus * phase
    return np.cos(angles), np.sin(angles)


def conv_body(
    x_ref, c1_ref, s1_ref, twc_ref, tws_ref, vc_ref, vs_ref, vsum_ref, vdiff_ref, ci_ref, si_ref, o_ref,
    yre_ref, yim_ref,
):
    streams = x_ref.shape[0]
    group = streams // 2
    pad = c1_ref.shape[0]

    def dot(a, b):
        return jnp.dot(a, b, precision=PRECISION, preferred_element_type=jnp.float32)

    twc = twc_ref[...]
    tws = tws_ref[...]
    c1 = c1_ref[...]
    s1 = s1_ref[...]
    for j in range(streams):
        xj = x_ref[j]
        a = dot(c1, xj)
        b = dot(s1, xj)
        yre_ref[j * pad : (j + 1) * pad, :] = a * twc - b * tws
        yim_ref[j * pad : (j + 1) * pad, :] = a * tws + b * twc
    vc = vc_ref[...]
    vs = vs_ref[...]
    yre = yre_ref[...]
    yim = yim_ref[...]
    vsum = vsum_ref[...]
    ac = dot(yre, vc)
    bd = dot(yim, vs)
    zre = ac - bd
    zim = dot(yre + yim, vsum) - ac - bd
    half = group * pad
    pre = zre[:half] * zre[half:] - zim[:half] * zim[half:]
    pim = zre[:half] * zim[half:] + zim[:half] * zre[half:]
    vdiff = vdiff_ref[...]
    ac = dot(pre, vc)
    bd = dot(pim, vs)
    qre = ac + bd
    qim = dot(pre + pim, vdiff) - ac + bd
    ci = ci_ref[...]
    si = si_ref[...]
    for g in range(group):
        ure = qre[g * pad : (g + 1) * pad]
        uim = qim[g * pad : (g + 1) * pad]
        vre = ure * twc + uim * tws
        vim = uim * twc - ure * tws
        o_ref[g] = dot(ci, vre) - dot(si, vim)


def fused_kernel(shards, parts, src_ref, *refs):
    tables = refs[:10]
    out_ref, stage_ref = refs[10:12]
    recv_ref, x_ref, o_ref, yre_ref, yim_ref, sends, recvs, local = refs[12:]
    me = lax.axis_index("seq")
    row = lax.axis_index("ch")
    mesh_id = pl.DeviceIdType.MESH
    streams = x_ref.shape[0]
    size = streams // 2
    barrier = pltpu.get_barrier_semaphore()

    def peer_of(step):
        distance = step // 2 + 1
        sign = 1 - 2 * (step % 2)
        return lax.rem(me + sign * distance + shards, shards)

    def greet(step, carry):
        pl.semaphore_signal(barrier, inc=1, device_id=(peer_of(step), row), device_id_type=mesh_id)
        return carry

    lax.fori_loop(0, shards - 1, greet, 0)
    pl.semaphore_wait(barrier, shards - 1)

    def scatter(source, target, phase):
        own = pltpu.make_async_copy(source(me), target(me), local.at[phase])
        own.start()

        def copy_to(peer, slot):
            return pltpu.make_async_remote_copy(
                src_ref=source(peer),
                dst_ref=target(slot),
                send_sem=sends.at[phase, peer],
                recv_sem=recvs.at[phase, slot],
                device_id=(peer, row),
                device_id_type=mesh_id,
            )

        def send(step, carry):
            copy_to(peer_of(step), me).start()
            return carry

        lax.fori_loop(0, shards - 1, send, 0)

        def finish():
            def wait_one(step, carry):
                peer = peer_of(step)
                copy_to(peer, me).wait_send()
                copy_to(peer, peer).wait_recv()
                return carry

            lax.fori_loop(0, shards - 1, wait_one, 0)
            own.wait()

        return finish

    arrivals = [
        scatter(
            lambda j, h=h: src_ref.at[j, :, pl.ds(h * size, size), :],
            lambda j, h=h: recv_ref.at[j, h],
            h,
        )
        for h in range(parts)
    ]
    returns = []
    for h in range(parts):
        arrivals[h]()
        gathers = [
            pltpu.make_async_copy(
                recv_ref.at[:, h, j // size, j % size, :], x_ref.at[j], local.at[2 * parts + j]
            )
            for j in range(streams)
        ]
        for copy in gathers:
            copy.start()
        for copy in gathers:
            copy.wait()
        conv_body(x_ref, *tables, o_ref, yre_ref, yim_ref)
        put = pltpu.make_async_copy(o_ref, stage_ref.at[h], local.at[2 * parts + streams])
        put.start()
        put.wait()
        returns.append(
            scatter(
                lambda j, h=h: stage_ref.at[h, :, j, :],
                lambda j, h=h: out_ref.at[j, pl.ds(h * size, size), :],
                parts + h,
            )
        )
    for finish in returns:
        finish()


def long_conv(pieces, parts):
    blocks, _, channels, rows = pieces.shape
    group = channels // parts
    streams = 2 * group
    coarse = 2 * blocks
    total = coarse * rows
    half = blocks + 1
    pad = -(-half // 8) * 8
    live = (np.arange(pad) < half).astype(np.float64)
    c1, s1 = phase_table(pad, blocks, coarse, -1.0)
    c1 = c1 * live[:, None]
    s1 = s1 * live[:, None]
    twc, tws = phase_table(pad, rows, total, -1.0)
    vc, vs = phase_table(rows, rows, rows, -1.0)
    k1 = np.arange(pad)
    weight = np.where((k1 == 0) | (k1 == blocks), 1.0, 2.0) * live / total
    ci, si = phase_table(blocks, pad, coarse, 1.0)
    ci = ci * weight[None, :]
    si = si * weight[None, :]
    tables = [c1, s1, twc, tws, vc, vs, vc + vs, vc - vs, ci, si]
    tables = [jnp.asarray(t, dtype=jnp.float32) for t in tables]
    vmem = pl.BlockSpec(memory_space=pltpu.VMEM)
    anywhere = pl.BlockSpec(memory_space=pl.ANY)
    f32 = jnp.float32
    return pl.pallas_call(
        functools.partial(fused_kernel, blocks, parts),
        out_shape=[
            jax.ShapeDtypeStruct((blocks, channels, rows), f32),
            jax.ShapeDtypeStruct((parts, group, blocks, rows), f32),
        ],
        in_specs=[anywhere] + [vmem] * len(tables),
        out_specs=[anywhere] * 2,
        scratch_shapes=[
            pltpu.VMEM((blocks, parts, 2, group, rows), f32),
            pltpu.VMEM((streams, blocks, rows), f32),
            pltpu.VMEM((group, blocks, rows), f32),
            pltpu.VMEM((streams * pad, rows), f32),
            pltpu.VMEM((streams * pad, rows), f32),
            pltpu.SemaphoreType.DMA((2 * parts, blocks)),
            pltpu.SemaphoreType.DMA((2 * parts, blocks)),
            pltpu.SemaphoreType.DMA((2 * parts + streams + 1,)),
        ],
        compiler_params=pltpu.CompilerParams(collective_id=0, has_side_effects=True),
    )(pieces, *tables)[0]


def shifted(block, axis, distance):
    devices = range(lax.axis_size(axis))
    route = [(i - distance, i) for i in devices if i - distance in devices]
    return lax.ppermute(block, axis, route)


def on_device(qkv, short_w, skip, filt):
    rows, _, width = qkv.shape
    taps = short_w.shape[0]
    shards = lax.axis_size("seq")
    group = width // shards
    rim = shifted(qkv[rows - (taps - 1) :], "seq", 1)
    extended = jnp.concatenate([rim, qkv], axis=0).astype(jnp.float32)
    feat = short_w[0] * extended[taps - 1 : taps - 1 + rows]
    for tap in range(1, taps):
        feat = feat + short_w[tap] * extended[taps - 1 - tap : taps - 1 - tap + rows]
    query = feat[:, 0, :]
    signal = feat[:, 1, :] * feat[:, 2, :]
    source = jnp.stack([signal, filt]).reshape(2, rows, shards, group).transpose(2, 0, 3, 1)
    values = long_conv(source, 2)
    conv = values.reshape(width, rows).T
    return (query * (conv + skip * signal)).astype(jnp.bfloat16)


def solution(mesh):
    return jax.shard_map(
        on_device,
        mesh=mesh,
        in_specs=(P("seq", None, "ch"), P(None, None, "ch"), P("ch"), P("seq", "ch")),
        out_specs=P("seq", "ch"),
        check_vma=False,
    )
```

```python
import functools
import math

import jax
import numpy as np
import jax.numpy as jnp
from jax import lax
from jax.experimental import pallas as pl
from jax.experimental.pallas import tpu as pltpu
from jax.sharding import PartitionSpec as P

PRECISION = lax.Precision.HIGHEST


def phase_table(count_out, count_in, modulus, sign):
    phase = np.arange(count_out)[:, None] * np.arange(count_in)[None, :] % modulus
    angles = sign * 2.0 * np.pi / modulus * phase
    return np.cos(angles), np.sin(angles)


def conv_body(
    x_ref, c1_ref, s1_ref, twc_ref, tws_ref, vc_ref, vs_ref, vsum_ref, vdiff_ref, ci_ref, si_ref, o_ref,
    yre_ref, yim_ref,
):
    streams = x_ref.shape[0]
    group = streams // 2
    pad = c1_ref.shape[0]

    def dot(a, b):
        return jnp.dot(a, b, precision=PRECISION, preferred_element_type=jnp.float32)

    twc = twc_ref[...]
    tws = tws_ref[...]
    c1 = c1_ref[...]
    s1 = s1_ref[...]
    for j in range(streams):
        xj = x_ref[j]
        a = dot(c1, xj)
        b = dot(s1, xj)
        yre_ref[j * pad : (j + 1) * pad, :] = a * twc - b * tws
        yim_ref[j * pad : (j + 1) * pad, :] = a * tws + b * twc
    vc = vc_ref[...]
    vs = vs_ref[...]
    yre = yre_ref[...]
    yim = yim_ref[...]
    vsum = vsum_ref[...]
    ac = dot(yre, vc)
    bd = dot(yim, vs)
    zre = ac - bd
    zim = dot(yre + yim, vsum) - ac - bd
    half = group * pad
    pre = zre[:half] * zre[half:] - zim[:half] * zim[half:]
    pim = zre[:half] * zim[half:] + zim[:half] * zre[half:]
    vdiff = vdiff_ref[...]
    ac = dot(pre, vc)
    bd = dot(pim, vs)
    qre = ac + bd
    qim = dot(pre + pim, vdiff) - ac + bd
    ci = ci_ref[...]
    si = si_ref[...]
    for g in range(group):
        ure = qre[g * pad : (g + 1) * pad]
        uim = qim[g * pad : (g + 1) * pad]
        vre = ure * twc + uim * tws
        vim = uim * twc - ure * tws
        o_ref[g] = dot(ci, vre) - dot(si, vim)


def fused_kernel(shards, parts, src_ref, *refs):
    tables = refs[:10]
    out_ref = refs[10]
    recv_ref, x_ref, o_all, yre_ref, yim_ref, sends, recvs, local = refs[11:]
    me = lax.axis_index("seq")
    row = lax.axis_index("ch")
    mesh_id = pl.DeviceIdType.MESH
    streams = x_ref.shape[0]
    size = streams // 2
    barrier = pltpu.get_barrier_semaphore()

    def peer_of(step):
        distance = step // 2 + 1
        sign = 1 - 2 * (step % 2)
        return lax.rem(me + sign * distance + shards, shards)

    def greet(step, carry):
        pl.semaphore_signal(barrier, inc=1, device_id=(peer_of(step), row), device_id_type=mesh_id)
        return carry

    lax.fori_loop(0, shards - 1, greet, 0)
    pl.semaphore_wait(barrier, shards - 1)

    def scatter(source, target, phase):
        own = pltpu.make_async_copy(source(me), target(me), local.at[phase])
        own.start()

        def copy_to(peer, slot):
            return pltpu.make_async_remote_copy(
                src_ref=source(peer),
                dst_ref=target(slot),
                send_sem=sends.at[phase, peer],
                recv_sem=recvs.at[phase, slot],
                device_id=(peer, row),
                device_id_type=mesh_id,
            )

        def send(step, carry):
            copy_to(peer_of(step), me).start()
            return carry

        lax.fori_loop(0, shards - 1, send, 0)

        def finish():
            def wait_one(step, carry):
                peer = peer_of(step)
                copy_to(peer, me).wait_send()
                copy_to(peer, peer).wait_recv()
                return carry

            lax.fori_loop(0, shards - 1, wait_one, 0)
            own.wait()

        return finish

    arrivals = [
        scatter(
            lambda j, h=h: src_ref.at[j, :, pl.ds(h * size, size), :],
            lambda j, h=h: recv_ref.at[j, h],
            h,
        )
        for h in range(parts)
    ]
    returns = []
    for h in range(parts):
        arrivals[h]()
        gathers = [
            pltpu.make_async_copy(
                recv_ref.at[:, h, j // size, j % size, :], x_ref.at[j], local.at[2 * parts + j]
            )
            for j in range(streams)
        ]
        for copy in gathers:
            copy.start()
        for copy in gathers:
            copy.wait()
        conv_body(x_ref, *tables, o_all.at[h], yre_ref, yim_ref)
        returns.append(
            scatter(
                lambda j, h=h: o_all.at[h, :, j, :],
                lambda j, h=h: out_ref.at[j, pl.ds(h * size, size), :],
                parts + h,
            )
        )
    for finish in returns:
        finish()


def long_conv(pieces, parts):
    blocks, _, channels, rows = pieces.shape
    group = channels // parts
    streams = 2 * group
    coarse = 2 * blocks
    total = coarse * rows
    half = blocks + 1
    pad = -(-half // 8) * 8
    live = (np.arange(pad) < half).astype(np.float64)
    c1, s1 = phase_table(pad, blocks, coarse, -1.0)
    c1 = c1 * live[:, None]
    s1 = s1 * live[:, None]
    twc, tws = phase_table(pad, rows, total, -1.0)
    vc, vs = phase_table(rows, rows, rows, -1.0)
    k1 = np.arange(pad)
    weight = np.where((k1 == 0) | (k1 == blocks), 1.0, 2.0) * live / total
    ci, si = phase_table(blocks, pad, coarse, 1.0)
    ci = ci * weight[None, :]
    si = si * weight[None, :]
    tables = [c1, s1, twc, tws, vc, vs, vc + vs, vc - vs, ci, si]
    tables = [jnp.asarray(t, dtype=jnp.float32) for t in tables]
    vmem = pl.BlockSpec(memory_space=pltpu.VMEM)
    anywhere = pl.BlockSpec(memory_space=pl.ANY)
    f32 = jnp.float32
    return pl.pallas_call(
        functools.partial(fused_kernel, blocks, parts),
        out_shape=[
            jax.ShapeDtypeStruct((blocks, channels, rows), f32),
        ],
        in_specs=[anywhere] + [vmem] * len(tables),
        out_specs=[anywhere],
        scratch_shapes=[
            pltpu.VMEM((blocks, parts, 2, group, rows), f32),
            pltpu.VMEM((streams, blocks, rows), f32),
            pltpu.VMEM((parts, group, blocks, rows), f32),
            pltpu.VMEM((streams * pad, rows), f32),
            pltpu.VMEM((streams * pad, rows), f32),
            pltpu.SemaphoreType.DMA((2 * parts, blocks)),
            pltpu.SemaphoreType.DMA((2 * parts, blocks)),
            pltpu.SemaphoreType.DMA((2 * parts + streams + 1,)),
        ],
        compiler_params=pltpu.CompilerParams(collective_id=0, has_side_effects=True),
    )(pieces, *tables)[0]


def shifted(block, axis, distance):
    devices = range(lax.axis_size(axis))
    route = [(i - distance, i) for i in devices if i - distance in devices]
    return lax.ppermute(block, axis, route)


def on_device(qkv, short_w, skip, filt):
    rows, _, width = qkv.shape
    taps = short_w.shape[0]
    shards = lax.axis_size("seq")
    group = width // shards
    rim = shifted(qkv[rows - (taps - 1) :], "seq", 1)
    extended = jnp.concatenate([rim, qkv], axis=0).astype(jnp.float32)
    feat = short_w[0] * extended[taps - 1 : taps - 1 + rows]
    for tap in range(1, taps):
        feat = feat + short_w[tap] * extended[taps - 1 - tap : taps - 1 - tap + rows]
    query = feat[:, 0, :]
    signal = feat[:, 1, :] * feat[:, 2, :]
    source = jnp.stack([signal, filt]).reshape(2, rows, shards, group).transpose(2, 0, 3, 1)
    values = long_conv(source, 2)
    conv = values.reshape(width, rows).T
    return (query * (conv + skip * signal)).astype(jnp.bfloat16)


def solution(mesh):
    return jax.shard_map(
        on_device,
        mesh=mesh,
        in_specs=(P("seq", None, "ch"), P(None, None, "ch"), P("ch"), P("seq", "ch")),
        out_specs=P("seq", "ch"),
        check_vma=False,
    )
```

```python
import functools
import math

import jax
import numpy as np
import jax.numpy as jnp
from jax import lax
from jax.experimental import pallas as pl
from jax.experimental.pallas import tpu as pltpu
from jax.sharding import PartitionSpec as P

PRECISION = lax.Precision.HIGHEST


def phase_table(count_out, count_in, modulus, sign):
    phase = np.arange(count_out)[:, None] * np.arange(count_in)[None, :] % modulus
    angles = sign * 2.0 * np.pi / modulus * phase
    return np.cos(angles), np.sin(angles)


def conv_body(
    x_ref, c1_ref, s1_ref, twc_ref, tws_ref, vc_ref, vs_ref, vsum_ref, vdiff_ref, ci_ref, si_ref, o_ref,
    yre_ref, yim_ref,
):
    streams = len(x_ref)
    group = streams // 2
    pad = c1_ref.shape[0]

    def dot(a, b):
        return jnp.dot(a, b, precision=PRECISION, preferred_element_type=jnp.float32)

    twc = twc_ref[...]
    tws = tws_ref[...]
    c1 = c1_ref[...]
    s1 = s1_ref[...]
    for j in range(streams):
        xj = x_ref[j][...]
        a = dot(c1, xj)
        b = dot(s1, xj)
        yre_ref[j * pad : (j + 1) * pad, :] = a * twc - b * tws
        yim_ref[j * pad : (j + 1) * pad, :] = a * tws + b * twc
    vc = vc_ref[...]
    vs = vs_ref[...]
    yre = yre_ref[...]
    yim = yim_ref[...]
    vsum = vsum_ref[...]
    ac = dot(yre, vc)
    bd = dot(yim, vs)
    zre = ac - bd
    zim = dot(yre + yim, vsum) - ac - bd
    half = group * pad
    pre = zre[:half] * zre[half:] - zim[:half] * zim[half:]
    pim = zre[:half] * zim[half:] + zim[:half] * zre[half:]
    vdiff = vdiff_ref[...]
    ac = dot(pre, vc)
    bd = dot(pim, vs)
    qre = ac + bd
    qim = dot(pre + pim, vdiff) - ac + bd
    ci = ci_ref[...]
    si = si_ref[...]
    for g in range(group):
        ure = qre[g * pad : (g + 1) * pad]
        uim = qim[g * pad : (g + 1) * pad]
        vre = ure * twc + uim * tws
        vim = uim * twc - ure * tws
        o_ref[g] = dot(ci, vre) - dot(si, vim)


def fused_kernel(shards, parts, src_ref, *refs):
    tables = refs[:10]
    out_ref = refs[10]
    x_all, o_all, yre_ref, yim_ref, sends, recvs, local = refs[11:]
    me = lax.axis_index("seq")
    row = lax.axis_index("ch")
    mesh_id = pl.DeviceIdType.MESH
    size = x_all.shape[2]
    streams = 2 * size
    barrier = pltpu.get_barrier_semaphore()

    def peer_of(step):
        distance = step // 2 + 1
        sign = 1 - 2 * (step % 2)
        return lax.rem(me + sign * distance + shards, shards)

    def greet(step, carry):
        pl.semaphore_signal(barrier, inc=1, device_id=(peer_of(step), row), device_id_type=mesh_id)
        return carry

    lax.fori_loop(0, shards - 1, greet, 0)
    pl.semaphore_wait(barrier, shards - 1)

    def scatter(source, target, phase):
        own = pltpu.make_async_copy(source(me), target(me), local.at[phase])
        own.start()

        def copy_to(peer, slot):
            return pltpu.make_async_remote_copy(
                src_ref=source(peer),
                dst_ref=target(slot),
                send_sem=sends.at[phase, peer],
                recv_sem=recvs.at[phase, slot],
                device_id=(peer, row),
                device_id_type=mesh_id,
            )

        def send(step, carry):
            copy_to(peer_of(step), me).start()
            return carry

        lax.fori_loop(0, shards - 1, send, 0)

        def finish():
            def wait_one(step, carry):
                peer = peer_of(step)
                copy_to(peer, me).wait_send()
                copy_to(peer, peer).wait_recv()
                return carry

            lax.fori_loop(0, shards - 1, wait_one, 0)
            own.wait()

        return finish

    arrivals = [
        scatter(
            lambda j, h=h: src_ref.at[j, :, pl.ds(h * size, size), :],
            lambda j, h=h: x_all.at[h, :, :, j, :],
            h,
        )
        for h in range(parts)
    ]
    returns = []
    for h in range(parts):
        arrivals[h]()
        x_ref = [x_all.at[h, s, g] for s in range(2) for g in range(size)]
        conv_body(x_ref, *tables, o_all.at[h], yre_ref, yim_ref)
        returns.append(
            scatter(
                lambda j, h=h: o_all.at[h, :, j, :],
                lambda j, h=h: out_ref.at[j, pl.ds(h * size, size), :],
                parts + h,
            )
        )
    for finish in returns:
        finish()


def long_conv(pieces, parts):
    blocks, _, channels, rows = pieces.shape
    group = channels // parts
    streams = 2 * group
    coarse = 2 * blocks
    total = coarse * rows
    half = blocks + 1
    pad = -(-half // 8) * 8
    live = (np.arange(pad) < half).astype(np.float64)
    c1, s1 = phase_table(pad, blocks, coarse, -1.0)
    c1 = c1 * live[:, None]
    s1 = s1 * live[:, None]
    twc, tws = phase_table(pad, rows, total, -1.0)
    vc, vs = phase_table(rows, rows, rows, -1.0)
    k1 = np.arange(pad)
    weight = np.where((k1 == 0) | (k1 == blocks), 1.0, 2.0) * live / total
    ci, si = phase_table(blocks, pad, coarse, 1.0)
    ci = ci * weight[None, :]
    si = si * weight[None, :]
    tables = [c1, s1, twc, tws, vc, vs, vc + vs, vc - vs, ci, si]
    tables = [jnp.asarray(t, dtype=jnp.float32) for t in tables]
    vmem = pl.BlockSpec(memory_space=pltpu.VMEM)
    anywhere = pl.BlockSpec(memory_space=pl.ANY)
    f32 = jnp.float32
    return pl.pallas_call(
        functools.partial(fused_kernel, blocks, parts),
        out_shape=[
            jax.ShapeDtypeStruct((blocks, channels, rows), f32),
        ],
        in_specs=[anywhere] + [vmem] * len(tables),
        out_specs=[anywhere],
        scratch_shapes=[
            pltpu.VMEM((parts, 2, group, blocks, rows), f32),
            pltpu.VMEM((parts, group, blocks, rows), f32),
            pltpu.VMEM((streams * pad, rows), f32),
            pltpu.VMEM((streams * pad, rows), f32),
            pltpu.SemaphoreType.DMA((2 * parts, blocks)),
            pltpu.SemaphoreType.DMA((2 * parts, blocks)),
            pltpu.SemaphoreType.DMA((2 * parts + streams + 1,)),
        ],
        compiler_params=pltpu.CompilerParams(collective_id=0, has_side_effects=True),
    )(pieces, *tables)[0]


def shifted(block, axis, distance):
    devices = range(lax.axis_size(axis))
    route = [(i - distance, i) for i in devices if i - distance in devices]
    return lax.ppermute(block, axis, route)


def on_device(qkv, short_w, skip, filt):
    rows, _, width = qkv.shape
    taps = short_w.shape[0]
    shards = lax.axis_size("seq")
    group = width // shards
    rim = shifted(qkv[rows - (taps - 1) :], "seq", 1)
    extended = jnp.concatenate([rim, qkv], axis=0).astype(jnp.float32)
    feat = short_w[0] * extended[taps - 1 : taps - 1 + rows]
    for tap in range(1, taps):
        feat = feat + short_w[tap] * extended[taps - 1 - tap : taps - 1 - tap + rows]
    query = feat[:, 0, :]
    signal = feat[:, 1, :] * feat[:, 2, :]
    source = jnp.stack([signal, filt]).reshape(2, rows, shards, group).transpose(2, 0, 3, 1)
    values = long_conv(source, 2)
    conv = values.reshape(width, rows).T
    return (query * (conv + skip * signal)).astype(jnp.bfloat16)


def solution(mesh):
    return jax.shard_map(
        on_device,
        mesh=mesh,
        in_specs=(P("seq", None, "ch"), P(None, None, "ch"), P("ch"), P("seq", "ch")),
        out_specs=P("seq", "ch"),
        check_vma=False,
    )
```

```python
import functools
import math

import jax
import numpy as np
import jax.numpy as jnp
from jax import lax
from jax.experimental import pallas as pl
from jax.experimental.pallas import tpu as pltpu
from jax.sharding import PartitionSpec as P

PRECISION = lax.Precision.HIGHEST


def phase_table(count_out, count_in, modulus, sign):
    phase = np.arange(count_out)[:, None] * np.arange(count_in)[None, :] % modulus
    angles = sign * 2.0 * np.pi / modulus * phase
    return np.cos(angles), np.sin(angles)


def conv_body(
    x_ref, c1_ref, s1_ref, twc_ref, tws_ref, vc_ref, vs_ref, vsum_ref, vdiff_ref, ci_ref, si_ref, o_ref,
    yre_ref, yim_ref,
):
    streams = len(x_ref)
    group = streams // 2
    pad = c1_ref.shape[0]

    def dot(a, b):
        return jnp.dot(a, b, precision=PRECISION, preferred_element_type=jnp.float32)

    twc = twc_ref[...]
    tws = tws_ref[...]
    c1 = c1_ref[...]
    s1 = s1_ref[...]
    for j in range(streams):
        xj = x_ref[j][...]
        a = dot(c1, xj)
        b = dot(s1, xj)
        yre_ref[j * pad : (j + 1) * pad, :] = a * twc - b * tws
        yim_ref[j * pad : (j + 1) * pad, :] = a * tws + b * twc
    vc = vc_ref[...]
    vs = vs_ref[...]
    yre = yre_ref[...]
    yim = yim_ref[...]
    vsum = vsum_ref[...]
    ac = dot(yre, vc)
    bd = dot(yim, vs)
    zre = ac - bd
    zim = dot(yre + yim, vsum) - ac - bd
    half = group * pad
    pre = zre[:half] * zre[half:] - zim[:half] * zim[half:]
    pim = zre[:half] * zim[half:] + zim[:half] * zre[half:]
    vdiff = vdiff_ref[...]
    ac = dot(pre, vc)
    bd = dot(pim, vs)
    qre = ac + bd
    qim = dot(pre + pim, vdiff) - ac + bd
    ci = ci_ref[...]
    si = si_ref[...]
    for g in range(group):
        ure = qre[g * pad : (g + 1) * pad]
        uim = qim[g * pad : (g + 1) * pad]
        vre = ure * twc + uim * tws
        vim = uim * twc - ure * tws
        o_ref[g] = dot(ci, vre) - dot(si, vim)


def fused_kernel(shards, parts, src_ref, *refs):
    tables = refs[:10]
    out_ref = refs[10]
    x_all, o_all, yre_ref, yim_ref, sends, recvs, local = refs[11:]
    me = lax.axis_index("seq")
    row = lax.axis_index("ch")
    mesh_id = pl.DeviceIdType.MESH
    size = x_all.shape[2]
    streams = 2 * size
    barrier = pltpu.get_barrier_semaphore()

    def peer_of(step):
        distance = step // 2 + 1
        sign = 1 - 2 * (step % 2)
        return lax.rem(me + sign * distance + shards, shards)

    def greet(step, carry):
        pl.semaphore_signal(barrier, inc=1, device_id=(peer_of(step), row), device_id_type=mesh_id)
        return carry

    lax.fori_loop(0, shards - 1, greet, 0)
    pl.semaphore_wait(barrier, shards - 1)

    def scatter(source, target, phase):
        own = pltpu.make_async_copy(source(me), target(me), local.at[phase])
        own.start()

        def copy_to(peer, slot):
            return pltpu.make_async_remote_copy(
                src_ref=source(peer),
                dst_ref=target(slot),
                send_sem=sends.at[phase, peer],
                recv_sem=recvs.at[phase, slot],
                device_id=(peer, row),
                device_id_type=mesh_id,
            )

        def send(step, carry):
            copy_to(peer_of(step), me).start()
            return carry

        lax.fori_loop(0, shards - 1, send, 0)

        def sent():
            def wait_one(step, carry):
                copy_to(peer_of(step), me).wait_send()
                return carry

            lax.fori_loop(0, shards - 1, wait_one, 0)

        def arrived():
            def wait_one(step, carry):
                peer = peer_of(step)
                copy_to(peer, peer).wait_recv()
                return carry

            lax.fori_loop(0, shards - 1, wait_one, 0)
            own.wait()

        return sent, arrived

    arrivals = []
    for h in range(parts):
        if h:
            arrivals[h - 1][0]()
        arrivals.append(
            scatter(
                lambda j, h=h: src_ref.at[j, :, pl.ds(h * size, size), :],
                lambda j, h=h: x_all.at[h, :, :, j, :],
                h,
            )
        )
    returns = []
    for h in range(parts):
        arrivals[h][1]()
        x_ref = [x_all.at[h, s, g] for s in range(2) for g in range(size)]
        conv_body(x_ref, *tables, o_all.at[h], yre_ref, yim_ref)
        returns.append(
            scatter(
                lambda j, h=h: o_all.at[h, :, j, :],
                lambda j, h=h: out_ref.at[j, pl.ds(h * size, size), :],
                parts + h,
            )
        )
    arrivals[-1][0]()
    for sent, arrived in returns:
        sent()
        arrived()


def long_conv(pieces, parts):
    blocks, _, channels, rows = pieces.shape
    group = channels // parts
    streams = 2 * group
    coarse = 2 * blocks
    total = coarse * rows
    half = blocks + 1
    pad = -(-half // 8) * 8
    live = (np.arange(pad) < half).astype(np.float64)
    c1, s1 = phase_table(pad, blocks, coarse, -1.0)
    c1 = c1 * live[:, None]
    s1 = s1 * live[:, None]
    twc, tws = phase_table(pad, rows, total, -1.0)
    vc, vs = phase_table(rows, rows, rows, -1.0)
    k1 = np.arange(pad)
    weight = np.where((k1 == 0) | (k1 == blocks), 1.0, 2.0) * live / total
    ci, si = phase_table(blocks, pad, coarse, 1.0)
    ci = ci * weight[None, :]
    si = si * weight[None, :]
    tables = [c1, s1, twc, tws, vc, vs, vc + vs, vc - vs, ci, si]
    tables = [jnp.asarray(t, dtype=jnp.float32) for t in tables]
    vmem = pl.BlockSpec(memory_space=pltpu.VMEM)
    anywhere = pl.BlockSpec(memory_space=pl.ANY)
    f32 = jnp.float32
    return pl.pallas_call(
        functools.partial(fused_kernel, blocks, parts),
        out_shape=[
            jax.ShapeDtypeStruct((blocks, channels, rows), f32),
        ],
        in_specs=[anywhere] + [vmem] * len(tables),
        out_specs=[anywhere],
        scratch_shapes=[
            pltpu.VMEM((parts, 2, group, blocks, rows), f32),
            pltpu.VMEM((parts, group, blocks, rows), f32),
            pltpu.VMEM((streams * pad, rows), f32),
            pltpu.VMEM((streams * pad, rows), f32),
            pltpu.SemaphoreType.DMA((2 * parts, blocks)),
            pltpu.SemaphoreType.DMA((2 * parts, blocks)),
            pltpu.SemaphoreType.DMA((2 * parts + streams + 1,)),
        ],
        compiler_params=pltpu.CompilerParams(collective_id=0, has_side_effects=True),
    )(pieces, *tables)[0]


def shifted(block, axis, distance):
    devices = range(lax.axis_size(axis))
    route = [(i - distance, i) for i in devices if i - distance in devices]
    return lax.ppermute(block, axis, route)


def on_device(qkv, short_w, skip, filt):
    rows, _, width = qkv.shape
    taps = short_w.shape[0]
    shards = lax.axis_size("seq")
    group = width // shards
    rim = shifted(qkv[rows - (taps - 1) :], "seq", 1)
    extended = jnp.concatenate([rim, qkv], axis=0).astype(jnp.float32)
    feat = short_w[0] * extended[taps - 1 : taps - 1 + rows]
    for tap in range(1, taps):
        feat = feat + short_w[tap] * extended[taps - 1 - tap : taps - 1 - tap + rows]
    query = feat[:, 0, :]
    signal = feat[:, 1, :] * feat[:, 2, :]
    source = jnp.stack([signal, filt]).reshape(2, rows, shards, group).transpose(2, 0, 3, 1)
    values = long_conv(source, 2)
    conv = values.reshape(width, rows).T
    return (query * (conv + skip * signal)).astype(jnp.bfloat16)


def solution(mesh):
    return jax.shard_map(
        on_device,
        mesh=mesh,
        in_specs=(P("seq", None, "ch"), P(None, None, "ch"), P("ch"), P("seq", "ch")),
        out_specs=P("seq", "ch"),
        check_vma=False,
    )
```

```python
import functools
import math

import jax
import numpy as np
import jax.numpy as jnp
from jax import lax
from jax.experimental import pallas as pl
from jax.experimental.pallas import tpu as pltpu
from jax.sharding import PartitionSpec as P

PRECISION = lax.Precision.HIGHEST


def phase_table(count_out, count_in, modulus, sign):
    phase = np.arange(count_out)[:, None] * np.arange(count_in)[None, :] % modulus
    angles = sign * 2.0 * np.pi / modulus * phase
    return np.cos(angles), np.sin(angles)


def conv_body(
    x_ref, c1_ref, s1_ref, twc_ref, tws_ref, vc_ref, vs_ref, vsum_ref, vdiff_ref, ci_ref, si_ref, o_ref,
    yre_ref, yim_ref,
):
    streams = len(x_ref)
    group = streams // 2
    pad = c1_ref.shape[0]

    def dot(a, b):
        return jnp.dot(a, b, precision=PRECISION, preferred_element_type=jnp.float32)

    twc = twc_ref[...]
    tws = tws_ref[...]
    c1 = c1_ref[...]
    s1 = s1_ref[...]
    for j in range(streams):
        xj = x_ref[j][...]
        a = dot(c1, xj)
        b = dot(s1, xj)
        yre_ref[j * pad : (j + 1) * pad, :] = a * twc - b * tws
        yim_ref[j * pad : (j + 1) * pad, :] = a * tws + b * twc
    vc = vc_ref[...]
    vs = vs_ref[...]
    yre = yre_ref[...]
    yim = yim_ref[...]
    vsum = vsum_ref[...]
    ac = dot(yre, vc)
    bd = dot(yim, vs)
    zre = ac - bd
    zim = dot(yre + yim, vsum) - ac - bd
    half = group * pad
    pre = zre[:half] * zre[half:] - zim[:half] * zim[half:]
    pim = zre[:half] * zim[half:] + zim[:half] * zre[half:]
    vdiff = vdiff_ref[...]
    ac = dot(pre, vc)
    bd = dot(pim, vs)
    qre = ac + bd
    qim = dot(pre + pim, vdiff) - ac + bd
    ci = ci_ref[...]
    si = si_ref[...]
    for g in range(group):
        ure = qre[g * pad : (g + 1) * pad]
        uim = qim[g * pad : (g + 1) * pad]
        vre = ure * twc + uim * tws
        vim = uim * twc - ure * tws
        o_ref[g] = dot(ci, vre) - dot(si, vim)


def fused_kernel(shards, parts, src_ref, *refs):
    tables = refs[:10]
    out_ref = refs[10]
    x_all, o_all, yre_ref, yim_ref, sends, recvs, local = refs[11:]
    me = lax.axis_index("seq")
    row = lax.axis_index("ch")
    mesh_id = pl.DeviceIdType.MESH
    size = x_all.shape[2]
    streams = 2 * size
    barrier = pltpu.get_barrier_semaphore()

    def peer_of(step):
        distance = step // 2 + 1
        sign = 1 - 2 * (step % 2)
        return lax.rem(me + sign * distance + shards, shards)

    def greet(step, carry):
        pl.semaphore_signal(barrier, inc=1, device_id=(peer_of(step), row), device_id_type=mesh_id)
        return carry

    lax.fori_loop(0, shards - 1, greet, 0)
    pl.semaphore_wait(barrier, shards - 1)

    def scatter(source, target, phase):
        own = pltpu.make_async_copy(source(me), target(me), local.at[phase])
        own.start()

        def copy_to(peer, slot):
            return pltpu.make_async_remote_copy(
                src_ref=source(peer),
                dst_ref=target(slot),
                send_sem=sends.at[phase, peer],
                recv_sem=recvs.at[phase, slot],
                device_id=(peer, row),
                device_id_type=mesh_id,
            )

        def send(step, carry):
            copy_to(peer_of(step), me).start()
            return carry

        lax.fori_loop(0, shards - 1, send, 0)

        def sent(first, last):
            def wait_one(step, carry):
                copy_to(peer_of(step), me).wait_send()
                return carry

            lax.fori_loop(first, last, wait_one, 0)

        def finish(first=0):
            sent(first, shards - 1)

            def wait_one(step, carry):
                peer = peer_of(step)
                copy_to(peer, peer).wait_recv()
                return carry

            lax.fori_loop(0, shards - 1, wait_one, 0)
            own.wait()

        return sent, finish

    early = shards // 2
    arrivals = []
    for h in range(parts):
        if h:
            arrivals[h - 1][0](0, early)
        arrivals.append(
            scatter(
                lambda j, h=h: src_ref.at[j, :, pl.ds(h * size, size), :],
                lambda j, h=h: x_all.at[h, :, :, j, :],
                h,
            )
        )
    returns = []
    for h in range(parts):
        arrivals[h][1](early if h < parts - 1 else 0)
        x_ref = [x_all.at[h, s, g] for s in range(2) for g in range(size)]
        conv_body(x_ref, *tables, o_all.at[h], yre_ref, yim_ref)
        returns.append(
            scatter(
                lambda j, h=h: o_all.at[h, :, j, :],
                lambda j, h=h: out_ref.at[j, pl.ds(h * size, size), :],
                parts + h,
            )
        )
    for _, finish in returns:
        finish()


def long_conv(pieces, parts):
    blocks, _, channels, rows = pieces.shape
    group = channels // parts
    streams = 2 * group
    coarse = 2 * blocks
    total = coarse * rows
    half = blocks + 1
    pad = -(-half // 8) * 8
    live = (np.arange(pad) < half).astype(np.float64)
    c1, s1 = phase_table(pad, blocks, coarse, -1.0)
    c1 = c1 * live[:, None]
    s1 = s1 * live[:, None]
    twc, tws = phase_table(pad, rows, total, -1.0)
    vc, vs = phase_table(rows, rows, rows, -1.0)
    k1 = np.arange(pad)
    weight = np.where((k1 == 0) | (k1 == blocks), 1.0, 2.0) * live / total
    ci, si = phase_table(blocks, pad, coarse, 1.0)
    ci = ci * weight[None, :]
    si = si * weight[None, :]
    tables = [c1, s1, twc, tws, vc, vs, vc + vs, vc - vs, ci, si]
    tables = [jnp.asarray(t, dtype=jnp.float32) for t in tables]
    vmem = pl.BlockSpec(memory_space=pltpu.VMEM)
    anywhere = pl.BlockSpec(memory_space=pl.ANY)
    f32 = jnp.float32
    return pl.pallas_call(
        functools.partial(fused_kernel, blocks, parts),
        out_shape=[
            jax.ShapeDtypeStruct((blocks, channels, rows), f32),
        ],
        in_specs=[anywhere] + [vmem] * len(tables),
        out_specs=[anywhere],
        scratch_shapes=[
            pltpu.VMEM((parts, 2, group, blocks, rows), f32),
            pltpu.VMEM((parts, group, blocks, rows), f32),
            pltpu.VMEM((streams * pad, rows), f32),
            pltpu.VMEM((streams * pad, rows), f32),
            pltpu.SemaphoreType.DMA((2 * parts, blocks)),
            pltpu.SemaphoreType.DMA((2 * parts, blocks)),
            pltpu.SemaphoreType.DMA((2 * parts + streams + 1,)),
        ],
        compiler_params=pltpu.CompilerParams(collective_id=0, has_side_effects=True),
    )(pieces, *tables)[0]


def shifted(block, axis, distance):
    devices = range(lax.axis_size(axis))
    route = [(i - distance, i) for i in devices if i - distance in devices]
    return lax.ppermute(block, axis, route)


def on_device(qkv, short_w, skip, filt):
    rows, _, width = qkv.shape
    taps = short_w.shape[0]
    shards = lax.axis_size("seq")
    group = width // shards
    rim = shifted(qkv[rows - (taps - 1) :], "seq", 1)
    extended = jnp.concatenate([rim, qkv], axis=0).astype(jnp.float32)
    feat = short_w[0] * extended[taps - 1 : taps - 1 + rows]
    for tap in range(1, taps):
        feat = feat + short_w[tap] * extended[taps - 1 - tap : taps - 1 - tap + rows]
    query = feat[:, 0, :]
    signal = feat[:, 1, :] * feat[:, 2, :]
    source = jnp.stack([signal, filt]).reshape(2, rows, shards, group).transpose(2, 0, 3, 1)
    values = long_conv(source, 2)
    conv = values.reshape(width, rows).T
    return (query * (conv + skip * signal)).astype(jnp.bfloat16)


def solution(mesh):
    return jax.shard_map(
        on_device,
        mesh=mesh,
        in_specs=(P("seq", None, "ch"), P(None, None, "ch"), P("ch"), P("seq", "ch")),
        out_specs=P("seq", "ch"),
        check_vma=False,
    )
```
